128 devices in a mesh: dp: 4 (over y), expert: 32 (over z, x, core).
Axes of the slice: x: 4, y: 4, z: 4, core: 2. Of those that a mesh axis runs over, the one named last changes fastest.
Arguments:
- tokens: bfloat16 [16384, 4096], P(('dp', 'expert')), may hold values from -6 to 6
- cotangent: bfloat16 [16384, 4096], P(('dp', 'expert')), may hold values from -25 to 25
- routes: int32 [16384, 2], P(('dp', 'expert')), may hold values from 0 to 31, all different within a row; in each aligned block of 128 rows (0 to 127, 128 to 255, ...) at most 16 rows name the same one
- route_gates: float32 [16384, 2], P(('dp', 'expert')), may hold values from 0.2 to 1
- norm_gain: float32 [4096], replicated, may hold values from 0.25 to 1.75
- gate_matrix: bfloat16 [32, 4096, 768], P('expert'), may hold values from -0.140625 to 0.140625
- up_matrix: bfloat16 [32, 4096, 768], P('expert'), may hold values from -0.140625 to 0.140625
- down_matrix: bfloat16 [32, 4096, 768], P('expert'), may hold values from -0.21650635 to 0.21650635
Outputs:
- input_grad: bfloat16 [16384, 4096], P(('dp', 'expert'))
- gain_grad: float32 [4096], P(('dp', 'expert'))
The draws below stay inside these ranges and needn't reach their ends.
Inputs may be any that keep to these rules, and one draw needn't show every extreme that they name: `routes`: each row names 2 different experts. In the rows of one device no expert is named more than 16 times, and in every draw some device's rows name some expert exactly 16 times.
All inputs are finite; a program needn't handle non-finite values.
Results may differ from the reference program's by a relative error of at most 0.0057.
Values may be sent and summed in bfloat16 or wider, within the bound.
A program may use at most 128 MiB of HBM per device.

```python
import math
import jax
import jax.numpy as jnp
import numpy as np
from jax import lax

D = 4096
FF = 768
TOPW = 2
TOK_DEV = 128
EXPERTS = 32
CAP = 16
TOKENS = 16384


def input_field(key):
    field_key = jax.random.fold_in(key, 1)
    values = jnp.clip(jax.random.normal(field_key, (TOKENS, D), jnp.float32), -6.0, 6.0)
    return values


def draw_tokens(key, part):
    return input_field(key).astype(jnp.bfloat16)


def draw_cotangent(key, part):
    field = input_field(key)
    sign_bits = jax.random.randint(jax.random.fold_in(key, 3), (TOKENS, 1), 0, 2)
    signs = (2 * sign_bits - 1).astype(jnp.float32)
    noise_key = jax.random.fold_in(key, 2)
    noise = jnp.clip(jax.random.normal(noise_key, (TOKENS, D), jnp.float32), -4.0, 4.0)
    blocks = TOKENS // TOK_DEV
    width = D // blocks
    pairing = jax.random.permutation(jax.random.fold_in(key, 4), blocks).astype(jnp.int32)
    boost = jnp.where(pairing[:, None] == jnp.arange(blocks, dtype=jnp.int32)[None, :], 4.0, 1.0).astype(jnp.float32)
    noise = (noise.reshape(blocks, TOK_DEV, blocks, width) * boost[:, None, :, None]).reshape(TOKENS, D)
    return (signs * 1.5 * field + noise).astype(jnp.bfloat16)


def expert_stack(key, own_tag, scale):
    own_key = jax.random.fold_in(key, own_tag)
    shared_key = jax.random.fold_in(key, own_tag + 1)
    shared = jnp.clip(jax.random.normal(shared_key, (D, FF), jnp.float32), -4.0, 4.0)
    own = jnp.clip(jax.random.normal(own_key, (EXPERTS, D, FF), jnp.float32), -4.0, 4.0)
    return ((shared[None, :, :] + 0.5 * own) * (scale / math.sqrt(1.25))).astype(jnp.bfloat16)


def draw_gate_matrix(key, part):
    return expert_stack(key, 101, 1.5 / math.sqrt(D))


def draw_up_matrix(key, part):
    return expert_stack(key, 201, 1.5 / math.sqrt(D))


def draw_down_matrix(key, part):
    return expert_stack(key, 301, 1.0 / math.sqrt(FF))


def block_scale(key, dims, split, least, high):
    def one(dim, blocks):
        heights = jax.random.uniform(jax.random.fold_in(jax.random.fold_in(key, 6), dim), (blocks,), jnp.float32, least / len(split), high / len(split))
        return jnp.repeat(jnp.exp(heights), dims[dim] // blocks).reshape((-1,) + (1,) * (len(dims) - dim - 1))

    gain = one(*split[0])
    for cut in split[1:]:
        gain = gain * one(*cut)
    return gain


def deal_out(key, own, number, rows, count, top, most, skew):
    sequence = jax.random.permutation(key, count)
    packed, ordinary = portions_of(count, rows * top, most, skew, True), portions_of(count, rows * top, most, skew, False)
    places = jnp.arange(count)

    def named(sizes, offset_by):
        used = int((sizes > 0).sum())
        fixed = max(1, used // 4)
        shifted = fixed + (places - fixed + offset_by * (used - fixed)) % max(1, count - fixed)
        return jnp.zeros((count,), jnp.int32).at[sequence[jnp.where(places < fixed, places, shifted)]].set(jnp.asarray(sizes, jnp.int32))

    sizes = jnp.where(number % 4 == 0, named(packed, number // 4), named(ordinary, number - number // 4 - 1))
    mixed = jax.random.permutation(jax.random.fold_in(own, 3), count)
    source_of, sink = mixed[0:count // 2 * 2:2], mixed[1:count // 2 * 2:2]
    margin = jnp.minimum(sizes[source_of] - 1, most - sizes[sink]) // 2
    margin = jnp.where((source_of == sequence[0]) | (sink == sequence[0]) | (sizes[sink] == 0), 0, jnp.maximum(margin, 0))
    shifted = jax.random.randint(jax.random.fold_in(own, 4), (count // 2,), 0, 1 << 20) % (margin + 1)
    sizes = sizes.at[source_of].add(-shifted).at[sink].add(shifted)
    labels = jnp.searchsorted(jnp.cumsum(sizes), jnp.arange(rows * top), side="right").astype(jnp.int32)
    table = labels.reshape(top, rows).T
    table = table[jax.random.permutation(jax.random.fold_in(own, 1), rows)]
    offset_by = jax.random.randint(jax.random.fold_in(own, 2), (rows, 1), 0, top)
    return jnp.take_along_axis(table, (jnp.arange(top)[None, :] + offset_by) % top, axis=1)


def portions_of(amount, total, most, lean, full):
    loads = [(1 << 20) // math.isqrt(grade ** lean) + 1 for grade in range(1, amount + 1)]
    largest = most if full else min(most, max(-(-total // amount), total * loads[0] // sum(loads)))
    least = 1 if total - largest >= amount - 1 else 0
    counts, spare = [largest] + [least] * (amount - 1), total - largest - least * (amount - 1)
    while spare > 0:
        movable = [i for i in range(1, amount) if counts[i] < largest] or [i for i in range(1, amount) if counts[i] < most]
        pool, budget = sum([loads[i] for i in movable]), spare
        for i in movable:
            more = min(most - counts[i], max(1, budget * loads[i] // pool), spare)
            counts[i] = counts[i] + more
            spare = spare - more
    return np.array(counts)


def setup_inputs(seed: int = 0) -> dict:
    seeds = jax.random.split(jax.random.key(seed), 9)
    tokens = draw_tokens(jax.random.fold_in(seeds[8], 71), 0)
    cotangent = draw_cotangent(jax.random.fold_in(seeds[8], 71), 0)
    routes_keys = jax.random.split(jax.random.fold_in(seeds[2], 1), TOKENS // TOK_DEV)
    routes_turns = jax.random.permutation(jax.random.fold_in(seeds[2], 3), TOKENS // TOK_DEV)
    routes = jax.vmap(lambda own, number: deal_out(jax.random.fold_in(seeds[2], 2), own, number, TOK_DEV, EXPERTS, TOPW, CAP, 2))(routes_keys, routes_turns).reshape((TOKENS, TOPW))
    route_gates = jnp.clip(jnp.exp(math.log(1.0) - 1.609438 * jax.random.uniform(seeds[3], (TOKENS, TOPW), jnp.float32) ** block_scale(seeds[3], (TOKENS, TOPW), ((0, 128),), -0.2, 0.2)), 0.2, 1.0)
    norm_gain = jnp.clip(1.0 + 0.15 * jax.random.normal(seeds[4], (D,), jnp.float32), 0.25, 1.75)
    gate_matrix = draw_gate_matrix(jax.random.fold_in(seeds[8], 71), 0)
    up_matrix = draw_up_matrix(jax.random.fold_in(seeds[8], 71), 0)
    down_matrix = draw_down_matrix(jax.random.fold_in(seeds[8], 71), 0)
    return {"tokens": tokens, "cotangent": cotangent, "routes": routes, "route_gates": route_gates, "norm_gain": norm_gain, "gate_matrix": gate_matrix, "up_matrix": up_matrix, "down_matrix": down_matrix}


def reference(tokens, cotangent, routes, route_gates, norm_gain, gate_matrix, up_matrix, down_matrix):
    token_count = tokens.shape[0]
    features = tokens.shape[1]
    top_routes = routes.shape[1]
    experts = gate_matrix.shape[0]
    blocks = token_count // TOK_DEV
    flat_ids = routes.reshape(blocks, TOK_DEV * top_routes)
    onehot = (flat_ids[:, :, None] == jnp.arange(experts, dtype=jnp.int32)[None, None, :]).astype(jnp.int32)
    before = jnp.cumsum(onehot, axis=1) - onehot
    ranks = lax.optimization_barrier(jnp.sum(before * onehot, axis=2))
    slot_of = (jnp.arange(blocks, dtype=jnp.int32)[:, None] * CAP + ranks).reshape(-1).astype(jnp.int32)
    owner_ids = routes.reshape(-1).astype(jnp.int32)
    token_of = jnp.repeat(jnp.arange(token_count, dtype=jnp.int32), top_routes)
    slot_count = blocks * CAP
    slot_token = jnp.full((experts, slot_count), token_count, dtype=jnp.int32).at[owner_ids, slot_of].set(token_of)
    slot_gate = jnp.zeros((experts, slot_count), jnp.float32).at[owner_ids, slot_of].set(route_gates.reshape(-1))
    padded_tokens = jnp.concatenate([tokens, jnp.zeros((1, features), tokens.dtype)], axis=0)

    def project(slot_rows, gate_local, up_local):
        expert_rows = padded_tokens[slot_rows]
        pre_gate = jnp.dot(expert_rows, gate_local, preferred_element_type=jnp.float32)
        pre_up = jnp.dot(expert_rows, up_local, preferred_element_type=jnp.float32)
        return (pre_gate, pre_up)

    def forward(combined, inputs):
        slot_rows, route_scale, gate_local, up_local, down_local = inputs
        pre_gate, pre_up = project(slot_rows, gate_local, up_local)
        sigmoid_gate = jax.nn.sigmoid(pre_gate)
        hidden = (pre_gate * sigmoid_gate * pre_up).astype(jnp.bfloat16)
        expert_out = lax.dot_general(hidden, down_local, (((1,), (1,)), ((), ())), preferred_element_type=jnp.float32).astype(jnp.bfloat16)
        return (combined.at[slot_rows].add(route_scale[:, None] * expert_out.astype(jnp.float32)), None)
    combined, _ = lax.scan(forward, jnp.zeros((token_count + 1, features), jnp.float32), (slot_token, slot_gate, gate_matrix, up_matrix, down_matrix))
    residual = tokens.astype(jnp.float32) + combined[:token_count]
    inverse_rms = lax.rsqrt(lax.optimization_barrier(jnp.mean(residual * residual, axis=1, keepdims=True)) + 1e-06)
    normed = residual * inverse_rms
    upstream = cotangent.astype(jnp.float32)
    gain_grad = lax.optimization_barrier(jnp.sum(upstream * normed, axis=0))
    scaled = upstream * norm_gain[None, :]
    resid_grad = inverse_rms * (scaled - normed * lax.optimization_barrier(jnp.mean(scaled * normed, axis=1, keepdims=True)))
    padded_grad = jnp.concatenate([resid_grad, jnp.zeros((1, features), jnp.float32)], axis=0)

    def backward(grad_sum, inputs):
        slot_rows, route_scale, gate_local, up_local, down_local = inputs
        pre_gate, pre_up = project(slot_rows, gate_local, up_local)
        sigmoid_gate = jax.nn.sigmoid(pre_gate)
        route_grad = (route_scale[:, None] * padded_grad[slot_rows]).astype(jnp.bfloat16)
        hidden_grad = jnp.dot(route_grad, down_local, preferred_element_type=jnp.float32)
        gate_grad = (hidden_grad * pre_up * sigmoid_gate * (1.0 + pre_gate * (1.0 - sigmoid_gate))).astype(jnp.bfloat16)
        up_grad = (hidden_grad * pre_gate * sigmoid_gate).astype(jnp.bfloat16)
        row_grad = lax.dot_general(gate_grad, gate_local, (((1,), (1,)), ((), ())), preferred_element_type=jnp.float32)
        row_grad = row_grad + lax.dot_general(up_grad, up_local, (((1,), (1,)), ((), ())), preferred_element_type=jnp.float32)
        row_grad = row_grad.astype(jnp.bfloat16)
        return (grad_sum.at[slot_rows].add(row_grad.astype(jnp.float32)), None)
    moe_grad, _ = lax.scan(backward, jnp.zeros((token_count + 1, features), jnp.float32), (slot_token, slot_gate, gate_matrix, up_matrix, down_matrix))
    input_grad = (resid_grad + moe_grad[:token_count]).astype(jnp.bfloat16)
    return (input_grad, gain_grad)
```

```python
import functools
import jax
import jax.numpy as jnp
from jax import lax
from jax.experimental import pallas as pl
from jax.experimental.pallas import tpu as pltpu
from jax.sharding import PartitionSpec as P

MESH = pl.DeviceIdType.MESH
CHUNKS = 8
F32 = jnp.float32
BF16 = jnp.bfloat16
NT = (((1,), (1,)), ((), ()))


def peer_offsets():
    offsets = [(dz, dx, dc) for dz in range(4) for dx in range(4) for dc in range(2)][1:]
    near = lambda d: min(d, 4 - d)
    return sorted(offsets, key=lambda o: -(near(o[0]) + near(o[1])))


def dot(a, b):
    return jnp.dot(a, b, preferred_element_type=F32)


def kernel(
    dims,
    tokens, cotangent, routes, gates, gain, gate_w, up_w, down_w,
    out, gain_out,
    send_src, recv_exp, send_exp, recv_src,
    tok, cot, wg, wu, wd,
    residual, acc_a, acc_b, acc_c, half_a, half_b, place, pick, obuf,
    gsend, grecv, gsum, gall,
    load_sem, weight_sem, out_sem, send_sem, recv_sem, gain_sem,
):
    rows, features, inner, experts, cap, dps = dims
    slots = experts * cap
    width = features // CHUNKS
    me = lax.axis_index("expert")
    dp = lax.axis_index("dp")
    z, x, c = me // 8, (me // 2) % 4, me % 2
    peers = [
        ((z + dz) % 4) * 8 + ((x + dx) % 4) * 2 + (c + dc) % 2 for dz, dx, dc in peer_offsets()
    ]

    def cols(k):
        return pl.ds(pl.multiple_of(k * width, width), width)

    def block(e):
        return pl.ds(pl.multiple_of(e * cap, cap), cap)

    def tok_copy(k):
        return pltpu.make_async_copy(tokens.at[:, cols(k)], tok.at[k], load_sem.at[0, k])

    def cot_copy(k):
        return pltpu.make_async_copy(cotangent.at[:, cols(k)], cot.at[k], load_sem.at[1, k])

    def weight_copy(which, k):
        src, dst = ((gate_w, wg), (up_w, wu), (down_w, wd))[which]
        return pltpu.make_async_copy(src.at[cols(k), :], dst.at[k], weight_sem.at[which, k])

    def out_copy(k):
        return pltpu.make_async_copy(obuf.at[k], out.at[:, cols(k)], out_sem.at[k])

    barrier = pltpu.get_barrier_semaphore()
    for t in peers:
        pl.semaphore_signal(barrier, inc=1, device_id=(dp, t), device_id_type=MESH)
    for s in range(1, dps):
        pl.semaphore_signal(barrier, inc=1, device_id=((dp + s) % dps, me), device_id_type=MESH)

    for k in range(CHUNKS):
        tok_copy(k).start()
    for k in range(CHUNKS):
        weight_copy(0, k).start()
        weight_copy(1, k).start()
    for k in range(CHUNKS):
        weight_copy(2, k).start()
    for k in range(CHUNKS):
        cot_copy(k).start()

    sub = lax.broadcasted_iota(jnp.int32, (rows, rows), 0)
    lane = lax.broadcasted_iota(jnp.int32, (rows, rows), 1)
    lane_f = lane.astype(F32)
    named = routes[...].astype(F32)
    named_col = [named[:, j : j + 1] for j in range(2)]
    named_row = [
        jnp.sum(jnp.where(sub == lane, named_col[j], 0.0), axis=0, keepdims=True) for j in range(2)
    ]
    hot_col = [jnp.where(named_col[j] == lane_f, 1.0, 0.0) for j in range(2)]
    earlier = jnp.where(lane < sub, 1.0, 0.0).astype(BF16)
    before_col = dot(earlier, (hot_col[0] + hot_col[1]).astype(BF16))
    sub_f = sub.astype(F32)
    hot_row = [jnp.where(named_row[j] == sub_f, 1.0, 0.0) for j in range(2)]
    later = jnp.where(sub < lane, 1.0, 0.0).astype(BF16)
    before_row = dot((hot_row[0] + hot_row[1]).astype(BF16), later)
    slot_lane = lax.broadcasted_iota(jnp.int32, (rows, slots), 1).astype(F32)
    slot_sub = lax.broadcasted_iota(jnp.int32, (slots, rows), 0).astype(F32)
    for j in range(2):
        slot_col = named_col[j] * cap + jnp.sum(before_col * hot_col[j], axis=1, keepdims=True)
        slot_row = named_row[j] * cap + jnp.sum(before_row * hot_row[j], axis=0, keepdims=True)
        pick[pl.ds(j * rows, rows), :] = jnp.where(slot_col == slot_lane, 1.0, 0.0).astype(BF16)
        place[:, pl.ds(j * rows, rows)] = jnp.where(slot_row == slot_sub, 1.0, 0.0).astype(BF16)

    pl.semaphore_wait(barrier, experts - 1 + dps - 1)

    def send(phase, k, src, dst):
        pltpu.make_async_copy(
            src.at[k, block(me)], dst.at[k, block(me)], recv_sem.at[phase, k]
        ).start()
        for t in peers:
            pltpu.make_async_remote_copy(
                src_ref=src.at[k, block(t)],
                dst_ref=dst.at[k, block(me)],
                send_sem=send_sem.at[phase, k],
                recv_sem=recv_sem.at[phase, k],
                device_id=(dp, t),
                device_id_type=MESH,
            ).start()

    def wait_recv(phase, k, dst):
        pltpu.make_async_copy(dst.at[k], dst.at[k], recv_sem.at[phase, k]).wait()

    def wait_send(phase, k, src):
        part = src.at[k, pl.ds(0, slots - cap)]
        pltpu.make_async_copy(part, part, send_sem.at[phase, k]).wait()

    def stream(phase, make, src, dst):
        make(0)

        def step(k, carry):
            make(k)
            send(phase, k - 1, src, dst)
            return carry

        lax.fori_loop(1, CHUNKS, step, 0)
        send(phase, CHUNKS - 1, src, dst)

    both = place[:, pl.ds(0, rows)] + place[:, pl.ds(rows, rows)]

    def make_rows(k):
        tok_copy(k).wait()
        send_src[k] = dot(both, tok[k]).astype(BF16)

    stream(0, make_rows, send_src, recv_exp)

    acc_a[...] = jnp.zeros_like(acc_a)
    acc_b[...] = jnp.zeros_like(acc_b)
    acc_c[...] = jnp.zeros_like(acc_c)

    def project(k, carry):
        weight_copy(0, k).wait()
        weight_copy(1, k).wait()
        wait_recv(0, k, recv_exp)
        acc_a[...] += dot(recv_exp[k], wg[k])
        acc_b[...] += dot(recv_exp[k], wu[k])
        return carry

    lax.fori_loop(0, CHUNKS, project, 0)
    pre_gate = acc_a[...]
    half_a[...] = (pre_gate * jax.nn.sigmoid(pre_gate) * acc_b[...]).astype(BF16)

    def make_out(k):
        weight_copy(2, k).wait()
        send_exp[k] = lax.dot_general(
            half_a[...], wd[k], NT, preferred_element_type=F32
        ).astype(BF16)

    stream(1, make_out, send_exp, recv_src)

    scale = gates[...]
    scale = [scale[:, j : j + 1] for j in range(2)]

    def combine(k, carry):
        squares, products = carry
        cot_copy(k).wait()
        wait_recv(1, k, recv_src)
        taken = dot(pick[...], recv_src[k])
        row = tok[k].astype(F32) + (scale[0] * taken[:rows] + scale[1] * taken[rows:])
        residual[k] = row
        scaled = cot[k].astype(F32) * gain[:, cols(k)]
        squares = squares + jnp.sum(row * row, axis=1, keepdims=True)
        products = products + jnp.sum(scaled * row, axis=1, keepdims=True)
        return squares, products

    zero = jnp.zeros((rows, 1), F32)
    squares, products = lax.fori_loop(0, CHUNKS, combine, (zero, zero))
    inverse = lax.rsqrt(squares * (1.0 / features) + 1e-06)
    mean = products * inverse * (1.0 / features)

    per_dp = features // dps

    def make_grad(k):
        wait_send(0, k, send_src)
        normed = residual[k] * inverse
        upstream = cot[k].astype(F32)
        at = k * width
        gsend[at // per_dp, :, pl.ds(pl.multiple_of(at % per_dp, width), width)] = jnp.sum(
            upstream * normed, axis=0, keepdims=True
        )
        grad = inverse * (upstream * gain[:, cols(k)] - normed * mean)
        residual[k] = grad
        weighted = jnp.concatenate([scale[0] * grad, scale[1] * grad], axis=0).astype(BF16)
        send_src[k] = dot(place[...], weighted).astype(BF16)

    stream(2, make_grad, send_src, recv_exp)

    def gain_copy(s):
        other = (dp + s) % dps
        return pltpu.make_async_remote_copy(
            src_ref=gsend.at[other],
            dst_ref=grecv.at[dp],
            send_sem=gain_sem.at[0],
            recv_sem=gain_sem.at[1],
            device_id=(other, me),
            device_id_type=MESH,
        )

    for s in range(1, dps):
        gain_copy(s).start()
    grecv[dp] = gsend[dp]


    def take_grad(k, carry):
        wait_recv(2, k, recv_exp)
        acc_c[...] += dot(recv_exp[k], wd[k])
        return carry

    lax.fori_loop(0, CHUNKS, take_grad, 0)
    pre_gate = acc_a[...]
    sigmoid_gate = jax.nn.sigmoid(pre_gate)
    hidden_grad = acc_c[...]
    half_a[...] = (
        hidden_grad * acc_b[...] * sigmoid_gate * (1.0 + pre_gate * (1.0 - sigmoid_gate))
    ).astype(BF16)
    half_b[...] = (hidden_grad * pre_gate * sigmoid_gate).astype(BF16)

    def make_back(k):
        wait_send(1, k, send_exp)
        back = lax.dot_general(half_a[...], wg[k], NT, preferred_element_type=F32)
        back = back + lax.dot_general(half_b[...], wu[k], NT, preferred_element_type=F32)
        send_exp[k] = back.astype(BF16)

    stream(3, make_back, send_exp, recv_src)

    for s in range(1, dps):
        gain_copy(s).wait_send()
    arrived = grecv.at[pl.ds(0, dps - 1)]
    pltpu.make_async_copy(arrived, arrived, gain_sem.at[1]).wait()
    part = grecv[0]
    for s in range(1, dps):
        part = part + grecv[s]
    tiles = per_dp // 128
    each = experts // tiles
    for b in range(tiles):
        gsum[b] = part[:, b * 128 : (b + 1) * 128]

    def share_copy(t):
        return pltpu.make_async_remote_copy(
            src_ref=gsum.at[t // each],
            dst_ref=gall.at[me],
            send_sem=gain_sem.at[2],
            recv_sem=gain_sem.at[3],
            device_id=(dp, t),
            device_id_type=MESH,
        )

    for t in peers:
        share_copy(t).start()
    gall[me] = gsum[me // each]

    pair = pick[pl.ds(0, rows), :] + pick[pl.ds(rows, rows), :]

    def finish(k, carry):
        wait_recv(3, k, recv_src)
        obuf[k] = (residual[k] + dot(pair, recv_src[k])).astype(BF16)
        out_copy(k).start()
        return carry

    lax.fori_loop(0, CHUNKS, finish, 0)

    arrived = gall.at[pl.ds(0, experts - 1)]
    pltpu.make_async_copy(arrived, arrived, gain_sem.at[3]).wait()
    pltpu.make_async_copy(arrived, arrived, gain_sem.at[2]).wait()
    total = jnp.sum(gall[...], axis=0)
    lanes = 128 // each
    own = total
    for q in range(1, each):
        own = jnp.where(me % each == q, pltpu.roll(total, 128 - q * lanes, 1), own)
    gain_out[...] = own[:, :lanes]

    for k in range(CHUNKS):
        wait_send(2, k, send_src)
        wait_send(3, k, send_exp)
        out_copy(k).wait()


def shards(tokens, cotangent, routes, route_gates, norm_gain, gate_matrix, up_matrix, down_matrix):
    experts, dps = lax.axis_size("expert"), lax.axis_size("dp")
    rows, features = tokens.shape
    inner = gate_matrix.shape[2]
    cap = 2 * rows * routes.shape[1] // experts
    slots = experts * cap
    width = features // CHUNKS
    dims = (rows, features, inner, experts, cap, dps)
    anywhere = pl.BlockSpec(memory_space=pl.ANY)
    vmem = pl.BlockSpec(memory_space=pltpu.VMEM)
    dma = pltpu.SemaphoreType.DMA
    slab = lambda: pltpu.VMEM((CHUNKS, slots, width), BF16)
    weight = lambda: pltpu.VMEM((CHUNKS, width, inner), BF16)
    grads, gain_part = pl.pallas_call(
        functools.partial(kernel, dims),
        out_shape=(
            jax.ShapeDtypeStruct((rows, features), BF16),
            jax.ShapeDtypeStruct((1, features // (experts * dps)), F32),
        ),
        in_specs=[anywhere, anywhere, vmem, vmem, vmem, anywhere, anywhere, anywhere],
        out_specs=(anywhere, vmem),
        scratch_shapes=[
            slab(), slab(), slab(), slab(),
            pltpu.VMEM((CHUNKS, rows, width), BF16),
            pltpu.VMEM((CHUNKS, rows, width), BF16),
            weight(), weight(), weight(),
            pltpu.VMEM((CHUNKS, rows, width), F32),
            pltpu.VMEM((slots, inner), F32),
            pltpu.VMEM((slots, inner), F32),
            pltpu.VMEM((slots, inner), F32),
            pltpu.VMEM((slots, inner), BF16),
            pltpu.VMEM((slots, inner), BF16),
            pltpu.VMEM((slots, 2 * rows), BF16),
            pltpu.VMEM((2 * rows, slots), BF16),
            pltpu.VMEM((CHUNKS, rows, width), BF16),
            pltpu.VMEM((dps, 1, features // dps), F32),
            pltpu.VMEM((dps, 1, features // dps), F32),
            pltpu.VMEM((features // dps // 128, 1, 128), F32),
            pltpu.VMEM((experts, 1, 128), F32),
            dma((2, CHUNKS)),
            dma((3, CHUNKS)),
            dma((CHUNKS,)),
            dma((4, CHUNKS)),
            dma((4, CHUNKS)),
            dma((4,)),
        ],
        compiler_params=pltpu.CompilerParams(
            collective_id=0, has_side_effects=True, vmem_limit_bytes=63 * 2**20
        ),
        name="routed_experts",
    )(
        tokens, cotangent, routes, route_gates, norm_gain.reshape(1, features),
        gate_matrix[0], up_matrix[0], down_matrix[0],
    )
    return grads, gain_part.reshape(-1)


def solution(mesh):
    placed = (
        P(("dp", "expert"), None),
        P(("dp", "expert"), None),
        P(("dp", "expert"), None),
        P(("dp", "expert"), None),
        P(),
        P("expert", None, None),
        P("expert", None, None),
        P("expert", None, None),
    )
    return jax.shard_map(
        shards,
        mesh=mesh,
        in_specs=placed,
        out_specs=(P(("dp", "expert"), None), P(("dp", "expert"))),
        check_vma=False,
    )
```

```python
import functools
import jax
import jax.numpy as jnp
from jax import lax
from jax.experimental import pallas as pl
from jax.experimental.pallas import tpu as pltpu
from jax.sharding import PartitionSpec as P

MESH = pl.DeviceIdType.MESH
CHUNKS = 8
F32 = jnp.float32
BF16 = jnp.bfloat16
NT = (((1,), (1,)), ((), ()))


def peer_offsets():
    offsets = [(dz, dx, dc) for dz in range(4) for dx in range(4) for dc in range(2)][1:]
    near = lambda d: min(d, 4 - d)
    return sorted(offsets, key=lambda o: -(near(o[0]) + near(o[1])))


def dot(a, b):
    return jnp.dot(a, b, preferred_element_type=F32)


def kernel(
    dims,
    tokens, cotangent, routes, gates, gain, gate_w, up_w, down_w,
    out, gain_out,
    send_src, recv_exp, send_exp, recv_src,
    tok, cot, wg, wu, wd,
    residual, weighted, acc_a, acc_b, acc_c, half_a, half_b, place, pick, obuf,
    gsend, grecv, gsum, gall,
    load_sem, weight_sem, out_sem, send_sem, recv_sem, gain_sem,
):
    rows, features, inner, experts, cap, dps = dims
    half = experts * cap // 2
    width = features // CHUNKS
    me = lax.axis_index("expert")
    dp = lax.axis_index("dp")
    z, x, c = me // 8, (me // 2) % 4, me % 2
    groups = [
        [
            ((z + dz) % 4) * 8 + ((x + dx) % 4) * 2 + (c + dc) % 2
            for dz, dx, dc in peer_offsets()
            if dc == g
        ]
        for g in range(2)
    ]
    peers = groups[0] + groups[1]

    def cols(k):
        return pl.ds(pl.multiple_of(k * width, width), width)

    def block(e):
        return pl.ds(pl.multiple_of(e // 2 * cap, cap), cap)

    def tok_copy(k):
        return pltpu.make_async_copy(tokens.at[:, cols(k)], tok.at[k], load_sem.at[0, k])

    def cot_copy(k):
        return pltpu.make_async_copy(cotangent.at[:, cols(k)], cot.at[k], load_sem.at[1, k])

    def weight_copy(which, k):
        src, dst = ((gate_w, wg), (up_w, wu), (down_w, wd))[which]
        return pltpu.make_async_copy(src.at[cols(k), :], dst.at[k], weight_sem.at[which, k])

    def out_copy(k):
        return pltpu.make_async_copy(obuf.at[k], out.at[:, cols(k)], out_sem.at[k])

    barrier = pltpu.get_barrier_semaphore()
    for t in peers:
        pl.semaphore_signal(barrier, inc=1, device_id=(dp, t), device_id_type=MESH)
    for s in range(1, dps):
        pl.semaphore_signal(barrier, inc=1, device_id=((dp + s) % dps, me), device_id_type=MESH)

    for k in range(CHUNKS):
        tok_copy(k).start()
    for k in range(CHUNKS):
        weight_copy(0, k).start()
        weight_copy(1, k).start()
    for k in range(CHUNKS):
        weight_copy(2, k).start()
    for k in range(CHUNKS):
        cot_copy(k).start()

    sub = lax.broadcasted_iota(jnp.int32, (rows, rows), 0)
    lane = lax.broadcasted_iota(jnp.int32, (rows, rows), 1)
    lane_f, sub_f = lane.astype(F32), sub.astype(F32)

    def column(row):
        return jnp.sum(jnp.where(sub == lane, row, 0.0), axis=1, keepdims=True)

    named = routes[...].astype(F32)
    named_row = [named[j : j + 1, :] for j in range(2)]
    named_col = [column(row) for row in named_row]
    hot_col = [jnp.where(named_col[j] == lane_f, 1.0, 0.0) for j in range(2)]
    hot_row = [jnp.where(named_row[j] == sub_f, 1.0, 0.0) for j in range(2)]
    earlier = jnp.where(lane < sub, 1.0, 0.0).astype(BF16)
    later = jnp.where(sub < lane, 1.0, 0.0).astype(BF16)
    before_col = dot(earlier, (hot_col[0] + hot_col[1]).astype(BF16))
    before_row = dot((hot_row[0] + hot_row[1]).astype(BF16), later)
    core = c.astype(F32)

    def base(expert):
        chip = jnp.floor(expert * 0.5)
        return chip * cap + jnp.where(expert - 2.0 * chip == core, 0.0, float(half))

    slot_lane = lax.broadcasted_iota(jnp.int32, (rows, half), 1).astype(F32)
    slot_sub = lax.broadcasted_iota(jnp.int32, (half, rows), 0).astype(F32)
    for j in range(2):
        slot_col = base(named_col[j]) + jnp.sum(before_col * hot_col[j], axis=1, keepdims=True)
        slot_row = base(named_row[j]) + jnp.sum(before_row * hot_row[j], axis=0, keepdims=True)
        for g in range(2):
            at = pl.ds(j * rows, rows)
            pick[g, at, :] = jnp.where(slot_col - g * half == slot_lane, 1.0, 0.0).astype(BF16)
            place[g, :, at] = jnp.where(slot_row - g * half == slot_sub, 1.0, 0.0).astype(BF16)

    pl.semaphore_wait(barrier, experts - 1 + dps - 1)

    def send(phase, g, k, src, dst):
        if g == 0:
            pltpu.make_async_copy(
                src.at[g, k, block(me)], dst.at[g, k, block(me)], recv_sem.at[phase, g, k]
            ).start()
        for t in groups[g]:
            pltpu.make_async_remote_copy(
                src_ref=src.at[g, k, block(t)],
                dst_ref=dst.at[g, k, block(me)],
                send_sem=send_sem.at[phase, g, k],
                recv_sem=recv_sem.at[phase, g, k],
                device_id=(dp, t),
                device_id_type=MESH,
            ).start()

    def wait_recv(phase, g, k, dst):
        pltpu.make_async_copy(dst.at[g, k], dst.at[g, k], recv_sem.at[phase, g, k]).wait()

    def wait_send(phase, g, k, src):
        part = src.at[g, k, pl.ds(0, cap * len(groups[g]))]
        pltpu.make_async_copy(part, part, send_sem.at[phase, g, k]).wait()

    def stream(phase, g, make, src, dst):
        make(0)

        def step(k, carry):
            make(k)
            send(phase, g, k - 1, src, dst)
            return carry

        lax.fori_loop(1, CHUNKS, step, 0)
        send(phase, g, CHUNKS - 1, src, dst)

    for g in range(2):
        both = place[g, :, pl.ds(0, rows)] + place[g, :, pl.ds(rows, rows)]

        def make_rows(k):
            if g == 0:
                tok_copy(k).wait()
            send_src[g, k] = dot(both, tok[k]).astype(BF16)

        stream(0, g, make_rows, send_src, recv_exp)

    acc_a[...] = jnp.zeros_like(acc_a)
    acc_b[...] = jnp.zeros_like(acc_b)
    acc_c[...] = jnp.zeros_like(acc_c)

    for g in range(2):

        def project(k, carry):
            if g == 0:
                weight_copy(0, k).wait()
                weight_copy(1, k).wait()
            wait_recv(0, g, k, recv_exp)
            acc_a[g] += dot(recv_exp[g, k], wg[k])
            acc_b[g] += dot(recv_exp[g, k], wu[k])
            return carry

        lax.fori_loop(0, CHUNKS, project, 0)
        pre_gate = acc_a[g]
        half_a[g] = (pre_gate * jax.nn.sigmoid(pre_gate) * acc_b[g]).astype(BF16)

        def make_out(k):
            if g == 0:
                weight_copy(2, k).wait()
            send_exp[g, k] = lax.dot_general(
                half_a[g], wd[k], NT, preferred_element_type=F32
            ).astype(BF16)

        stream(1, g, make_out, send_exp, recv_src)

    scale = [column(gates[pl.ds(j, 1), :]) for j in range(2)]

    def take(g, k):
        taken = dot(pick[g], recv_src[g, k])
        return scale[0] * taken[:rows] + scale[1] * taken[rows:]

    def combine_first(k, carry):
        wait_recv(1, 0, k, recv_src)
        residual[k] = tok[k].astype(F32) + take(0, k)
        return carry

    lax.fori_loop(0, CHUNKS, combine_first, 0)

    def combine_last(k, carry):
        squares, products = carry
        cot_copy(k).wait()
        wait_recv(1, 1, k, recv_src)
        row = residual[k] + take(1, k)
        residual[k] = row
        scaled = cot[k].astype(F32) * gain[:, cols(k)]
        squares = squares + jnp.sum(row * row, axis=1, keepdims=True)
        products = products + jnp.sum(scaled * row, axis=1, keepdims=True)
        return squares, products

    zero = jnp.zeros((rows, 1), F32)
    squares, products = lax.fori_loop(0, CHUNKS, combine_last, (zero, zero))
    inverse = lax.rsqrt(squares * (1.0 / features) + 1e-06)
    mean = products * inverse * (1.0 / features)

    per_dp = features // dps
    for g in range(2):

        def make_grad(k):
            wait_send(0, g, k, send_src)
            if g == 0:
                normed = residual[k] * inverse
                upstream = cot[k].astype(F32)
                at = k * width
                gsend[at // per_dp, :, pl.ds(pl.multiple_of(at % per_dp, width), width)] = jnp.sum(
                    upstream * normed, axis=0, keepdims=True
                )
                grad = inverse * (upstream * gain[:, cols(k)] - normed * mean)
                residual[k] = grad
                for j in range(2):
                    weighted[k, pl.ds(j * rows, rows), :] = (scale[j] * grad).astype(BF16)
            send_src[g, k] = dot(place[g], weighted[k]).astype(BF16)

        stream(2, g, make_grad, send_src, recv_exp)

    def gain_copy(s):
        other = (dp + s) % dps
        return pltpu.make_async_remote_copy(
            src_ref=gsend.at[other],
            dst_ref=grecv.at[dp],
            send_sem=gain_sem.at[0],
            recv_sem=gain_sem.at[1],
            device_id=(other, me),
            device_id_type=MESH,
        )

    for s in range(1, dps):
        gain_copy(s).start()
    grecv[dp] = gsend[dp]

    for g in range(2):

        def take_grad(k, carry):
            wait_recv(2, g, k, recv_exp)
            acc_c[g] += dot(recv_exp[g, k], wd[k])
            return carry

        lax.fori_loop(0, CHUNKS, take_grad, 0)
        pre_gate = acc_a[g]
        sigmoid_gate = jax.nn.sigmoid(pre_gate)
        hidden_grad = acc_c[g]
        half_a[g] = (
            hidden_grad * acc_b[g] * sigmoid_gate * (1.0 + pre_gate * (1.0 - sigmoid_gate))
        ).astype(BF16)
        half_b[g] = (hidden_grad * pre_gate * sigmoid_gate).astype(BF16)

        def make_back(k):
            wait_send(1, g, k, send_exp)
            back = lax.dot_general(half_a[g], wg[k], NT, preferred_element_type=F32)
            back = back + lax.dot_general(half_b[g], wu[k], NT, preferred_element_type=F32)
            send_exp[g, k] = back.astype(BF16)

        stream(3, g, make_back, send_exp, recv_src)

    arrived = grecv.at[pl.ds(0, dps - 1)]
    for s in range(2):
        pltpu.make_async_copy(arrived, arrived, gain_sem.at[s]).wait()
    part = grecv[0]
    for s in range(1, dps):
        part = part + grecv[s]
    tiles = per_dp // 128
    each = experts // tiles
    for b in range(tiles):
        gsum[b] = part[:, b * 128 : (b + 1) * 128]

    for t in peers:
        pltpu.make_async_remote_copy(
            src_ref=gsum.at[t // each],
            dst_ref=gall.at[me],
            send_sem=gain_sem.at[2],
            recv_sem=gain_sem.at[3],
            device_id=(dp, t),
            device_id_type=MESH,
        ).start()
    gall[me] = gsum[me // each]

    def give(g, k):
        pair = pick[g, pl.ds(0, rows), :] + pick[g, pl.ds(rows, rows), :]
        wait_recv(3, g, k, recv_src)
        return residual[k] + dot(pair, recv_src[g, k])

    def finish_first(k, carry):
        residual[k] = give(0, k)
        return carry

    lax.fori_loop(0, CHUNKS, finish_first, 0)

    arrived = gall.at[pl.ds(0, experts - 1)]
    for s in range(2, 4):
        pltpu.make_async_copy(arrived, arrived, gain_sem.at[s]).wait()
    total = jnp.sum(gall[...], axis=0)
    lanes = 128 // each
    own = total
    for q in range(1, each):
        own = jnp.where(me % each == q, pltpu.roll(total, 128 - q * lanes, 1), own)
    gain_out[...] = own[:, :lanes]

    def finish_last(k, carry):
        obuf[k] = give(1, k).astype(BF16)
        out_copy(k).start()
        return carry

    lax.fori_loop(0, CHUNKS, finish_last, 0)

    for k in range(CHUNKS):
        for g in range(2):
            wait_send(2, g, k, send_src)
            wait_send(3, g, k, send_exp)
        out_copy(k).wait()


def shards(tokens, cotangent, routes, route_gates, norm_gain, gate_matrix, up_matrix, down_matrix):
    experts, dps = lax.axis_size("expert"), lax.axis_size("dp")
    rows, features = tokens.shape
    inner = gate_matrix.shape[2]
    cap = 2 * rows * routes.shape[1] // experts
    width = features // CHUNKS
    dims = (rows, features, inner, experts, cap, dps)
    anywhere = pl.BlockSpec(memory_space=pl.ANY)
    vmem = pl.BlockSpec(memory_space=pltpu.VMEM)
    dma = pltpu.SemaphoreType.DMA
    half = experts * cap // 2
    slab = lambda: pltpu.VMEM((2, CHUNKS, half, width), BF16)
    weight = lambda: pltpu.VMEM((CHUNKS, width, inner), BF16)
    grads, gain_part = pl.pallas_call(
        functools.partial(kernel, dims),
        out_shape=(
            jax.ShapeDtypeStruct((rows, features), BF16),
            jax.ShapeDtypeStruct((1, features // (experts * dps)), F32),
        ),
        in_specs=[anywhere, anywhere, vmem, vmem, vmem, anywhere, anywhere, anywhere],
        out_specs=(anywhere, vmem),
        scratch_shapes=[
            slab(), slab(), slab(), slab(),
            pltpu.VMEM((CHUNKS, rows, width), BF16),
            pltpu.VMEM((CHUNKS, rows, width), BF16),
            weight(), weight(), weight(),
            pltpu.VMEM((CHUNKS, rows, width), F32),
            pltpu.VMEM((CHUNKS, 2 * rows, width), BF16),
            pltpu.VMEM((2, half, inner), F32),
            pltpu.VMEM((2, half, inner), F32),
            pltpu.VMEM((2, half, inner), F32),
            pltpu.VMEM((2, half, inner), BF16),
            pltpu.VMEM((2, half, inner), BF16),
            pltpu.VMEM((2, half, 2 * rows), BF16),
            pltpu.VMEM((2, 2 * rows, half), BF16),
            pltpu.VMEM((CHUNKS, rows, width), BF16),
            pltpu.VMEM((dps, 1, features // dps), F32),
            pltpu.VMEM((dps, 1, features // dps), F32),
            pltpu.VMEM((features // dps // 128, 1, 128), F32),
            pltpu.VMEM((experts, 1, 128), F32),
            dma((2, CHUNKS)),
            dma((3, CHUNKS)),
            dma((CHUNKS,)),
            dma((4, 2, CHUNKS)),
            dma((4, 2, CHUNKS)),
            dma((4,)),
        ],
        compiler_params=pltpu.CompilerParams(
            collective_id=0, has_side_effects=True, vmem_limit_bytes=63 * 2**20
        ),
        name="routed_experts",
    )(
        tokens, cotangent, routes.T, route_gates.T, norm_gain.reshape(1, features),
        gate_matrix[0], up_matrix[0], down_matrix[0],
    )
    return grads, gain_part.reshape(-1)


def solution(mesh):
    placed = (
        P(("dp", "expert"), None),
        P(("dp", "expert"), None),
        P(("dp", "expert"), None),
        P(("dp", "expert"), None),
        P(),
        P("expert", None, None),
        P("expert", None, None),
        P("expert", None, None),
    )
    return jax.shard_map(
        shards,
        mesh=mesh,
        in_specs=placed,
        out_specs=(P(("dp", "expert"), None), P(("dp", "expert"))),
        check_vma=False,
    )
```

```python
import functools
import jax
import jax.numpy as jnp
from jax import lax
from jax.experimental import pallas as pl
from jax.experimental.pallas import tpu as pltpu
from jax.sharding import PartitionSpec as P

MESH = pl.DeviceIdType.MESH
CHUNKS = 8
F32 = jnp.float32
BF16 = jnp.bfloat16
NT = (((1,), (1,)), ((), ()))


def peer_offsets():
    offsets = [(dz, dx, dc) for dz in range(4) for dx in range(4) for dc in range(2)][1:]
    near = lambda d: min(d, 4 - d)
    return sorted(offsets, key=lambda o: -(near(o[0]) + near(o[1])))


def dot(a, b):
    return jnp.dot(a, b, preferred_element_type=F32)


def kernel(
    dims,
    tokens, cotangent, routes, gates, gain, gate_w, up_w, down_w,
    out, gain_out,
    send_src, recv_exp, send_exp, recv_src,
    tok, cot, wg, wu, wd,
    residual, acc_a, acc_b, acc_c, half_a, half_b, place, pick, obuf,
    gsend, grecv, gsum, gall,
    load_sem, weight_sem, out_sem, send_sem, recv_sem, gain_sem,
):
    rows, features, inner, experts, cap, dps = dims
    half = experts * cap // 2
    width = features // CHUNKS
    me = lax.axis_index("expert")
    dp = lax.axis_index("dp")
    z, x, c = me // 8, (me // 2) % 4, me % 2
    groups = [
        [
            ((z + dz) % 4) * 8 + ((x + dx) % 4) * 2 + (c + dc) % 2
            for dz, dx, dc in peer_offsets()
            if dc == g
        ]
        for g in range(2)
    ]
    peers = groups[0] + groups[1]

    def cols(k):
        return pl.ds(pl.multiple_of(k * width, width), width)

    def block(e):
        return pl.ds(pl.multiple_of(e // 2 * cap, cap), cap)

    def tok_copy(k):
        return pltpu.make_async_copy(tokens.at[:, cols(k)], tok.at[k], load_sem.at[0, k])

    def cot_copy(k):
        return pltpu.make_async_copy(cotangent.at[:, cols(k)], cot.at[k], load_sem.at[1, k])

    def weight_copy(which, k):
        src, dst = ((gate_w, wg), (up_w, wu), (down_w, wd))[which]
        return pltpu.make_async_copy(src.at[cols(k), :], dst.at[k], weight_sem.at[which, k])

    def out_copy(k):
        return pltpu.make_async_copy(obuf.at[k], out.at[:, cols(k)], out_sem.at[k])

    barrier = pltpu.get_barrier_semaphore()
    for t in peers:
        pl.semaphore_signal(barrier, inc=1, device_id=(dp, t), device_id_type=MESH)
    for s in range(1, dps):
        pl.semaphore_signal(barrier, inc=1, device_id=((dp + s) % dps, me), device_id_type=MESH)

    for k in range(CHUNKS):
        tok_copy(k).start()

    sub = lax.broadcasted_iota(jnp.int32, (rows, rows), 0)
    lane = lax.broadcasted_iota(jnp.int32, (rows, rows), 1)
    lane_f, sub_f = lane.astype(F32), sub.astype(F32)

    def column(row):
        return jnp.sum(jnp.where(sub == lane, row, 0.0), axis=1, keepdims=True)

    named = routes[...].astype(F32)
    named_row = [named[j : j + 1, :] for j in range(2)]
    hot_row = [jnp.where(named_row[j] == sub_f, 1.0, 0.0) for j in range(2)]
    later = jnp.where(sub < lane, 1.0, 0.0).astype(BF16)
    before_row = dot((hot_row[0] + hot_row[1]).astype(BF16), later)
    core = c.astype(F32)

    def base(expert):
        chip = jnp.floor(expert * 0.5)
        return chip * cap + jnp.where(expert - 2.0 * chip == core, 0.0, float(half))

    slot_sub = lax.broadcasted_iota(jnp.int32, (half, rows), 0).astype(F32)
    for j in range(2):
        slot_row = base(named_row[j]) + jnp.sum(before_row * hot_row[j], axis=0, keepdims=True)
        for g in range(2):
            place[g, :, pl.ds(j * rows, rows)] = jnp.where(slot_row - g * half == slot_sub, 1.0, 0.0).astype(BF16)

    pl.semaphore_wait(barrier, experts - 1 + dps - 1)

    def send(phase, g, k, src, dst):
        if g == 0:
            pltpu.make_async_copy(
                src.at[g, k, block(me)], dst.at[g, k, block(me)], recv_sem.at[phase, g, k]
            ).start()
        for t in groups[g]:
            pltpu.make_async_remote_copy(
                src_ref=src.at[g, k, block(t)],
                dst_ref=dst.at[g, k, block(me)],
                send_sem=send_sem.at[phase, g, k],
                recv_sem=recv_sem.at[phase, g, k],
                device_id=(dp, t),
                device_id_type=MESH,
            ).start()

    def wait_recv(phase, g, k, dst):
        pltpu.make_async_copy(dst.at[g, k], dst.at[g, k], recv_sem.at[phase, g, k]).wait()

    def wait_send(phase, g, k, src):
        part = src.at[g, k, pl.ds(0, cap * len(groups[g]))]
        pltpu.make_async_copy(part, part, send_sem.at[phase, g, k]).wait()

    def stream(phase, g, make, src, dst):
        make(0)

        def step(k, carry):
            make(k)
            send(phase, g, k - 1, src, dst)
            return carry

        lax.fori_loop(1, CHUNKS, step, 0)
        send(phase, g, CHUNKS - 1, src, dst)

    both = [place[g, :, pl.ds(0, rows)] + place[g, :, pl.ds(rows, rows)] for g in range(2)]

    def make_rows(k, carry):
        tok_copy(k).wait()
        for g in range(2):
            send_src[g, k] = dot(both[g], tok[k]).astype(BF16)
        send(0, 0, k, send_src, recv_exp)
        weight_copy(0, k).start()
        weight_copy(1, k).start()
        return carry

    lax.fori_loop(0, CHUNKS, make_rows, 0)

    def send_rows(k, carry):
        send(0, 1, k, send_src, recv_exp)
        weight_copy(2, k).start()
        cot_copy(k).start()
        return carry

    lax.fori_loop(0, CHUNKS, send_rows, 0)

    named_col = [column(row) for row in named_row]
    hot_col = [jnp.where(named_col[j] == lane_f, 1.0, 0.0) for j in range(2)]
    earlier = jnp.where(lane < sub, 1.0, 0.0).astype(BF16)
    before_col = dot(earlier, (hot_col[0] + hot_col[1]).astype(BF16))
    slot_lane = lax.broadcasted_iota(jnp.int32, (rows, half), 1).astype(F32)
    for j in range(2):
        slot_col = base(named_col[j]) + jnp.sum(before_col * hot_col[j], axis=1, keepdims=True)
        for g in range(2):
            hit = slot_col - g * half == slot_lane
            pick[g, pl.ds(j * rows, rows), :] = jnp.where(hit, 1.0, 0.0).astype(BF16)

    acc_a[...] = jnp.zeros_like(acc_a)
    acc_b[...] = jnp.zeros_like(acc_b)
    acc_c[...] = jnp.zeros_like(acc_c)

    for g in range(2):

        def project(k, carry):
            if g == 0:
                weight_copy(0, k).wait()
                weight_copy(1, k).wait()
            wait_recv(0, g, k, recv_exp)
            acc_a[g] += dot(recv_exp[g, k], wg[k])
            acc_b[g] += dot(recv_exp[g, k], wu[k])
            return carry

        lax.fori_loop(0, CHUNKS, project, 0)
        pre_gate = acc_a[g]
        half_a[g] = (pre_gate * jax.nn.sigmoid(pre_gate) * acc_b[g]).astype(BF16)

        def make_out(k):
            if g == 0:
                weight_copy(2, k).wait()
            send_exp[g, k] = lax.dot_general(
                half_a[g], wd[k], NT, preferred_element_type=F32
            ).astype(BF16)

        stream(1, g, make_out, send_exp, recv_src)

    scale = [column(gates[pl.ds(j, 1), :]) for j in range(2)]

    def take(g, k):
        taken = dot(pick[g], recv_src[g, k])
        return scale[0] * taken[:rows] + scale[1] * taken[rows:]

    def combine_first(k, carry):
        wait_recv(1, 0, k, recv_src)
        residual[k] = tok[k].astype(F32) + take(0, k)
        return carry

    lax.fori_loop(0, CHUNKS, combine_first, 0)

    def combine_last(k, carry):
        squares, products = carry
        cot_copy(k).wait()
        wait_recv(1, 1, k, recv_src)
        row = residual[k] + take(1, k)
        residual[k] = row
        scaled = cot[k].astype(F32) * gain[:, cols(k)]
        squares = squares + jnp.sum(row * row, axis=1, keepdims=True)
        products = products + jnp.sum(scaled * row, axis=1, keepdims=True)
        return squares, products

    zero = jnp.zeros((rows, 1), F32)
    squares, products = lax.fori_loop(0, CHUNKS, combine_last, (zero, zero))
    inverse = lax.rsqrt(squares * (1.0 / features) + 1e-06)
    mean = products * inverse * (1.0 / features)

    per_dp = features // dps

    def make_grad(k, carry):
        normed = residual[k] * inverse
        upstream = cot[k].astype(F32)
        at = k * width
        gsend[at // per_dp, :, pl.ds(pl.multiple_of(at % per_dp, width), width)] = jnp.sum(
            upstream * normed, axis=0, keepdims=True
        )
        grad = inverse * (upstream * gain[:, cols(k)] - normed * mean)
        residual[k] = grad
        rows_out = jnp.concatenate([scale[j] * grad for j in range(2)], axis=0).astype(BF16)
        for g in range(2):
            wait_send(0, g, k, send_src)
            send_src[g, k] = dot(place[g], rows_out).astype(BF16)
        send(2, 0, k, send_src, recv_exp)
        return carry

    lax.fori_loop(0, CHUNKS, make_grad, 0)

    def send_grad(k, carry):
        send(2, 1, k, send_src, recv_exp)
        return carry

    lax.fori_loop(0, CHUNKS, send_grad, 0)

    def gain_copy(s):
        other = (dp + s) % dps
        return pltpu.make_async_remote_copy(
            src_ref=gsend.at[other],
            dst_ref=grecv.at[dp],
            send_sem=gain_sem.at[0],
            recv_sem=gain_sem.at[1],
            device_id=(other, me),
            device_id_type=MESH,
        )

    for s in range(1, dps):
        gain_copy(s).start()
    grecv[dp] = gsend[dp]

    for g in range(2):

        def take_grad(k, carry):
            wait_recv(2, g, k, recv_exp)
            acc_c[g] += dot(recv_exp[g, k], wd[k])
            return carry

        lax.fori_loop(0, CHUNKS, take_grad, 0)
        pre_gate = acc_a[g]
        sigmoid_gate = jax.nn.sigmoid(pre_gate)
        hidden_grad = acc_c[g]
        half_a[g] = (
            hidden_grad * acc_b[g] * sigmoid_gate * (1.0 + pre_gate * (1.0 - sigmoid_gate))
        ).astype(BF16)
        half_b[g] = (hidden_grad * pre_gate * sigmoid_gate).astype(BF16)

        def make_back(k):
            wait_send(1, g, k, send_exp)
            back = lax.dot_general(half_a[g], wg[k], NT, preferred_element_type=F32)
            back = back + lax.dot_general(half_b[g], wu[k], NT, preferred_element_type=F32)
            send_exp[g, k] = back.astype(BF16)

        stream(3, g, make_back, send_exp, recv_src)

    arrived = grecv.at[pl.ds(0, dps - 1)]
    for s in range(2):
        pltpu.make_async_copy(arrived, arrived, gain_sem.at[s]).wait()
    part = grecv[0]
    for s in range(1, dps):
        part = part + grecv[s]
    tiles = per_dp // 128
    each = experts // tiles
    for b in range(tiles):
        gsum[b] = part[:, b * 128 : (b + 1) * 128]

    for t in peers:
        pltpu.make_async_remote_copy(
            src_ref=gsum.at[t // each],
            dst_ref=gall.at[me],
            send_sem=gain_sem.at[2],
            recv_sem=gain_sem.at[3],
            device_id=(dp, t),
            device_id_type=MESH,
        ).start()
    gall[me] = gsum[me // each]

    def give(g, k):
        pair = pick[g, pl.ds(0, rows), :] + pick[g, pl.ds(rows, rows), :]
        wait_recv(3, g, k, recv_src)
        return residual[k] + dot(pair, recv_src[g, k])

    def finish_first(k, carry):
        residual[k] = give(0, k)
        return carry

    lax.fori_loop(0, CHUNKS, finish_first, 0)

    arrived = gall.at[pl.ds(0, experts - 1)]
    for s in range(2, 4):
        pltpu.make_async_copy(arrived, arrived, gain_sem.at[s]).wait()
    total = jnp.sum(gall[...], axis=0)
    lanes = 128 // each
    own = total
    for q in range(1, each):
        own = jnp.where(me % each == q, pltpu.roll(total, 128 - q * lanes, 1), own)
    gain_out[...] = own[:, :lanes]

    def finish_last(k, carry):
        obuf[k] = give(1, k).astype(BF16)
        out_copy(k).start()
        return carry

    lax.fori_loop(0, CHUNKS, finish_last, 0)

    for k in range(CHUNKS):
        for g in range(2):
            wait_send(2, g, k, send_src)
            wait_send(3, g, k, send_exp)
        out_copy(k).wait()


def deliver(grads, gain_part, out, gain_out, buf, in_sem, out_sem):
    parts = buf.shape[0]
    rows = buf.shape[1]

    def load(i):
        return pltpu.make_async_copy(grads.at[pl.ds(i * rows, rows)], buf.at[i], in_sem.at[i])

    def store(i):
        return pltpu.make_async_copy(buf.at[i], out.at[pl.ds(i * rows, rows)], out_sem.at[i])

    for i in range(parts):
        load(i).start()
    gain_out[...] = gain_part[...]
    for i in range(parts):
        load(i).wait()
        store(i).start()
    for i in range(parts):
        store(i).wait()


def shards(tokens, cotangent, routes, route_gates, norm_gain, gate_matrix, up_matrix, down_matrix):
    experts, dps = lax.axis_size("expert"), lax.axis_size("dp")
    rows, features = tokens.shape
    inner = gate_matrix.shape[2]
    cap = 2 * rows * routes.shape[1] // experts
    width = features // CHUNKS
    dims = (rows, features, inner, experts, cap, dps)
    anywhere = pl.BlockSpec(memory_space=pl.ANY)
    vmem = pl.BlockSpec(memory_space=pltpu.VMEM)
    dma = pltpu.SemaphoreType.DMA
    half = experts * cap // 2
    slab = lambda: pltpu.VMEM((2, CHUNKS, half, width), BF16)
    weight = lambda: pltpu.VMEM((CHUNKS, width, inner), BF16)
    grads, gain_part = pl.pallas_call(
        functools.partial(kernel, dims),
        out_shape=(
            jax.ShapeDtypeStruct((rows, features), BF16),
            jax.ShapeDtypeStruct((1, features // (experts * dps)), F32),
        ),
        in_specs=[anywhere, anywhere, vmem, vmem, vmem, anywhere, anywhere, anywhere],
        out_specs=(anywhere, vmem),
        scratch_shapes=[
            slab(), slab(), slab(), slab(),
            pltpu.VMEM((CHUNKS, rows, width), BF16),
            pltpu.VMEM((CHUNKS, rows, width), BF16),
            weight(), weight(), weight(),
            pltpu.VMEM((CHUNKS, rows, width), F32),
            pltpu.VMEM((2, half, inner), F32),
            pltpu.VMEM((2, half, inner), F32),
            pltpu.VMEM((2, half, inner), F32),
            pltpu.VMEM((2, half, inner), BF16),
            pltpu.VMEM((2, half, inner), BF16),
            pltpu.VMEM((2, half, 2 * rows), BF16),
            pltpu.VMEM((2, 2 * rows, half), BF16),
            pltpu.VMEM((CHUNKS, rows, width), BF16),
            pltpu.VMEM((dps, 1, features // dps), F32),
            pltpu.VMEM((dps, 1, features // dps), F32),
            pltpu.VMEM((features // dps // 128, 1, 128), F32),
            pltpu.VMEM((experts, 1, 128), F32),
            dma((2, CHUNKS)),
            dma((3, CHUNKS)),
            dma((CHUNKS,)),
            dma((4, 2, CHUNKS)),
            dma((4, 2, CHUNKS)),
            dma((4,)),
        ],
        compiler_params=pltpu.CompilerParams(
            collective_id=0, has_side_effects=True, vmem_limit_bytes=63 * 2**20
        ),
        name="routed_experts",
    )(
        tokens, cotangent, routes.T, route_gates.T, norm_gain.reshape(1, features),
        gate_matrix[0], up_matrix[0], down_matrix[0],
    )
    grads, gain_part = pl.pallas_call(
        deliver,
        out_shape=(
            jax.ShapeDtypeStruct((rows, features), BF16),
            jax.ShapeDtypeStruct(gain_part.shape, F32),
        ),
        in_specs=[anywhere, vmem],
        out_specs=(anywhere, vmem),
        scratch_shapes=[
            pltpu.VMEM((4, rows // 4, features), BF16),
            dma((4,)),
            dma((4,)),
        ],
        compiler_params=pltpu.CompilerParams(vmem_limit_bytes=63 * 2**20),
        name="deliver",
    )(grads, gain_part)
    return grads, gain_part.reshape(-1)


def solution(mesh):
    placed = (
        P(("dp", "expert"), None),
        P(("dp", "expert"), None),
        P(("dp", "expert"), None),
        P(("dp", "expert"), None),
        P(),
        P("expert", None, None),
        P("expert", None, None),
        P("expert", None, None),
    )
    return jax.shard_map(
        shards,
        mesh=mesh,
        in_specs=placed,
        out_specs=(P(("dp", "expert"), None), P(("dp", "expert"))),
        check_vma=False,
    )
```

```python
import functools
import jax
import jax.numpy as jnp
from jax import lax
from jax.experimental import pallas as pl
from jax.experimental.pallas import tpu as pltpu
from jax.sharding import PartitionSpec as P

MESH = pl.DeviceIdType.MESH
CHUNKS = 8
F32 = jnp.float32
BF16 = jnp.bfloat16
NT = (((1,), (1,)), ((), ()))


def peer_offsets():
    offsets = [(dz, dx, dc) for dz in range(4) for dx in range(4) for dc in range(2)][1:]
    near = lambda d: min(d, 4 - d)
    return sorted(offsets, key=lambda o: -(near(o[0]) + near(o[1])))


def dot(a, b):
    return jnp.dot(a, b, preferred_element_type=F32)


def kernel(
    dims,
    tokens, cotangent, routes_in, gates_in, gain_in, gate_w, up_w, down_w,
    out, gain_out,
    send_src, recv_exp, send_exp, recv_src,
    tok, cot, routes, gates, gain, wg, wu, wd,
    residual, acc_a, acc_b, acc_c, half_a, half_b, place, pick,
    gsend, grecv, gsum, gall,
    load_sem, small_sem, weight_sem, send_sem, recv_sem, gain_sem,
):
    rows, features, inner, experts, cap, dps = dims
    half = experts * cap // 2
    width = features // CHUNKS
    me = lax.axis_index("expert")
    dp = lax.axis_index("dp")
    z, x, c = me // 8, (me // 2) % 4, me % 2
    groups = [
        [
            ((z + dz) % 4) * 8 + ((x + dx) % 4) * 2 + (c + dc) % 2
            for dz, dx, dc in peer_offsets()
            if dc == g
        ]
        for g in range(2)
    ]
    peers = groups[0] + groups[1]

    def cols(k):
        return pl.ds(pl.multiple_of(k * width, width), width)

    def block(e):
        return pl.ds(pl.multiple_of(e // 2 * cap, cap), cap)

    def tok_copy(k):
        return pltpu.make_async_copy(tokens.at[:, cols(k)], tok.at[k], load_sem.at[0, k])

    def cot_copy(k):
        return pltpu.make_async_copy(cotangent.at[:, cols(k)], cot.at[k], load_sem.at[1, k])

    def weight_copy(which, k):
        src, dst = ((gate_w, wg), (up_w, wu), (down_w, wd))[which]
        return pltpu.make_async_copy(src.at[cols(k), :], dst.at[k], weight_sem.at[which, k])

    barrier = pltpu.get_barrier_semaphore()
    for t in peers:
        pl.semaphore_signal(barrier, inc=1, device_id=(dp, t), device_id_type=MESH)
    for s in range(1, dps):
        pl.semaphore_signal(barrier, inc=1, device_id=((dp + s) % dps, me), device_id_type=MESH)

    small = [
        pltpu.make_async_copy(src, dst, small_sem.at[i])
        for i, (src, dst) in enumerate(((routes_in, routes), (gates_in, gates), (gain_in, gain)))
    ]
    for copy in small:
        copy.start()
    for k in range(CHUNKS):
        tok_copy(k).start()

    for copy in small:
        copy.wait()

    sub = lax.broadcasted_iota(jnp.int32, (rows, rows), 0)
    lane = lax.broadcasted_iota(jnp.int32, (rows, rows), 1)
    lane_f, sub_f = lane.astype(F32), sub.astype(F32)

    def column(row):
        return jnp.sum(jnp.where(sub == lane, row, 0.0), axis=1, keepdims=True)

    named = routes[...].astype(F32)
    named_row = [named[j : j + 1, :] for j in range(2)]
    hot_row = [jnp.where(named_row[j] == sub_f, 1.0, 0.0) for j in range(2)]
    later = jnp.where(sub < lane, 1.0, 0.0).astype(BF16)
    before_row = dot((hot_row[0] + hot_row[1]).astype(BF16), later)
    core = c.astype(F32)

    def base(expert):
        chip = jnp.floor(expert * 0.5)
        return chip * cap + jnp.where(expert - 2.0 * chip == core, 0.0, float(half))

    slot_sub = lax.broadcasted_iota(jnp.int32, (half, rows), 0).astype(F32)
    for j in range(2):
        slot_row = base(named_row[j]) + jnp.sum(before_row * hot_row[j], axis=0, keepdims=True)
        for g in range(2):
            place[g, :, pl.ds(j * rows, rows)] = jnp.where(slot_row - g * half == slot_sub, 1.0, 0.0).astype(BF16)

    pl.semaphore_wait(barrier, experts - 1 + dps - 1)

    def send(phase, g, k, src, dst):
        if g == 0:
            pltpu.make_async_copy(
                src.at[g, k, block(me)], dst.at[g, k, block(me)], recv_sem.at[phase, g, k]
            ).start()
        for t in groups[g]:
            pltpu.make_async_remote_copy(
                src_ref=src.at[g, k, block(t)],
                dst_ref=dst.at[g, k, block(me)],
                send_sem=send_sem.at[phase, g, k],
                recv_sem=recv_sem.at[phase, g, k],
                device_id=(dp, t),
                device_id_type=MESH,
            ).start()

    def wait_recv(phase, g, k, dst):
        pltpu.make_async_copy(dst.at[g, k], dst.at[g, k], recv_sem.at[phase, g, k]).wait()

    def wait_send(phase, g, k, src):
        part = src.at[g, k, pl.ds(0, cap * len(groups[g]))]
        pltpu.make_async_copy(part, part, send_sem.at[phase, g, k]).wait()

    def stream(phase, g, make, src, dst):
        make(0)

        def step(k, carry):
            make(k)
            send(phase, g, k - 1, src, dst)
            return carry

        lax.fori_loop(1, CHUNKS, step, 0)
        send(phase, g, CHUNKS - 1, src, dst)

    both = [place[g, :, pl.ds(0, rows)] + place[g, :, pl.ds(rows, rows)] for g in range(2)]

    def make_rows(k, carry):
        tok_copy(k).wait()
        for g in range(2):
            send_src[g, k] = dot(both[g], tok[k]).astype(BF16)
        send(0, 0, k, send_src, recv_exp)
        weight_copy(0, k).start()
        weight_copy(1, k).start()
        return carry

    lax.fori_loop(0, CHUNKS, make_rows, 0)

    def send_rows(k, carry):
        send(0, 1, k, send_src, recv_exp)
        weight_copy(2, k).start()
        cot_copy(k).start()
        return carry

    lax.fori_loop(0, CHUNKS, send_rows, 0)

    named_col = [column(row) for row in named_row]
    hot_col = [jnp.where(named_col[j] == lane_f, 1.0, 0.0) for j in range(2)]
    earlier = jnp.where(lane < sub, 1.0, 0.0).astype(BF16)
    before_col = dot(earlier, (hot_col[0] + hot_col[1]).astype(BF16))
    slot_lane = lax.broadcasted_iota(jnp.int32, (rows, half), 1).astype(F32)
    for j in range(2):
        slot_col = base(named_col[j]) + jnp.sum(before_col * hot_col[j], axis=1, keepdims=True)
        for g in range(2):
            hit = slot_col - g * half == slot_lane
            pick[g, pl.ds(j * rows, rows), :] = jnp.where(hit, 1.0, 0.0).astype(BF16)

    acc_a[...] = jnp.zeros_like(acc_a)
    acc_b[...] = jnp.zeros_like(acc_b)
    acc_c[...] = jnp.zeros_like(acc_c)

    for g in range(2):

        def project(k, carry):
            if g == 0:
                weight_copy(0, k).wait()
                weight_copy(1, k).wait()
            wait_recv(0, g, k, recv_exp)
            acc_a[g] += dot(recv_exp[g, k], wg[k])
            acc_b[g] += dot(recv_exp[g, k], wu[k])
            return carry

        lax.fori_loop(0, CHUNKS, project, 0)
        pre_gate = acc_a[g]
        half_a[g] = (pre_gate * jax.nn.sigmoid(pre_gate) * acc_b[g]).astype(BF16)

        def make_out(k):
            if g == 0:
                weight_copy(2, k).wait()
            send_exp[g, k] = lax.dot_general(
                half_a[g], wd[k], NT, preferred_element_type=F32
            ).astype(BF16)

        stream(1, g, make_out, send_exp, recv_src)

    scale = [column(gates[pl.ds(j, 1), :]) for j in range(2)]

    def take(g, k):
        taken = dot(pick[g], recv_src[g, k])
        return scale[0] * taken[:rows] + scale[1] * taken[rows:]

    def combine_first(k, carry):
        wait_recv(1, 0, k, recv_src)
        residual[k] = tok[k].astype(F32) + take(0, k)
        return carry

    lax.fori_loop(0, CHUNKS, combine_first, 0)

    def combine_last(k, carry):
        squares, products = carry
        cot_copy(k).wait()
        wait_recv(1, 1, k, recv_src)
        row = residual[k] + take(1, k)
        residual[k] = row
        scaled = cot[k].astype(F32) * gain[:, cols(k)]
        squares = squares + jnp.sum(row * row, axis=1, keepdims=True)
        products = products + jnp.sum(scaled * row, axis=1, keepdims=True)
        return squares, products

    zero = jnp.zeros((rows, 1), F32)
    squares, products = lax.fori_loop(0, CHUNKS, combine_last, (zero, zero))
    inverse = lax.rsqrt(squares * (1.0 / features) + 1e-06)
    mean = products * inverse * (1.0 / features)

    per_dp = features // dps

    def make_grad(k, carry):
        normed = residual[k] * inverse
        upstream = cot[k].astype(F32)
        at = k * width
        gsend[at // per_dp, :, pl.ds(pl.multiple_of(at % per_dp, width), width)] = jnp.sum(
            upstream * normed, axis=0, keepdims=True
        )
        grad = inverse * (upstream * gain[:, cols(k)] - normed * mean)
        residual[k] = grad
        rows_out = jnp.concatenate([scale[j] * grad for j in range(2)], axis=0).astype(BF16)
        for g in range(2):
            wait_send(0, g, k, send_src)
            send_src[g, k] = dot(place[g], rows_out).astype(BF16)
        send(2, 0, k, send_src, recv_exp)
        return carry

    lax.fori_loop(0, CHUNKS, make_grad, 0)

    def send_grad(k, carry):
        send(2, 1, k, send_src, recv_exp)
        return carry

    lax.fori_loop(0, CHUNKS, send_grad, 0)

    def gain_copy(s):
        other = (dp + s) % dps
        return pltpu.make_async_remote_copy(
            src_ref=gsend.at[other],
            dst_ref=grecv.at[dp],
            send_sem=gain_sem.at[0],
            recv_sem=gain_sem.at[1],
            device_id=(other, me),
            device_id_type=MESH,
        )

    for s in range(1, dps):
        gain_copy(s).start()
    grecv[dp] = gsend[dp]

    for g in range(2):

        def take_grad(k, carry):
            wait_recv(2, g, k, recv_exp)
            acc_c[g] += dot(recv_exp[g, k], wd[k])
            return carry

        lax.fori_loop(0, CHUNKS, take_grad, 0)
        pre_gate = acc_a[g]
        sigmoid_gate = jax.nn.sigmoid(pre_gate)
        hidden_grad = acc_c[g]
        half_a[g] = (
            hidden_grad * acc_b[g] * sigmoid_gate * (1.0 + pre_gate * (1.0 - sigmoid_gate))
        ).astype(BF16)
        half_b[g] = (hidden_grad * pre_gate * sigmoid_gate).astype(BF16)

        def make_back(k):
            wait_send(1, g, k, send_exp)
            back = lax.dot_general(half_a[g], wg[k], NT, preferred_element_type=F32)
            back = back + lax.dot_general(half_b[g], wu[k], NT, preferred_element_type=F32)
            send_exp[g, k] = back.astype(BF16)

        stream(3, g, make_back, send_exp, recv_src)

    arrived = grecv.at[pl.ds(0, dps - 1)]
    for s in range(2):
        pltpu.make_async_copy(arrived, arrived, gain_sem.at[s]).wait()
    part = grecv[0]
    for s in range(1, dps):
        part = part + grecv[s]
    tiles = per_dp // 128
    each = experts // tiles
    for b in range(tiles):
        gsum[b] = part[:, b * 128 : (b + 1) * 128]

    for t in peers:
        pltpu.make_async_remote_copy(
            src_ref=gsum.at[t // each],
            dst_ref=gall.at[me],
            send_sem=gain_sem.at[2],
            recv_sem=gain_sem.at[3],
            device_id=(dp, t),
            device_id_type=MESH,
        ).start()
    gall[me] = gsum[me // each]

    def give(g, k):
        pair = pick[g, pl.ds(0, rows), :] + pick[g, pl.ds(rows, rows), :]
        wait_recv(3, g, k, recv_src)
        return residual[k] + dot(pair, recv_src[g, k])

    def finish_first(k, carry):
        residual[k] = give(0, k)
        return carry

    lax.fori_loop(0, CHUNKS, finish_first, 0)

    arrived = gall.at[pl.ds(0, experts - 1)]
    for s in range(2, 4):
        pltpu.make_async_copy(arrived, arrived, gain_sem.at[s]).wait()
    total = jnp.sum(gall[...], axis=0)
    lanes = 128 // each
    own = total
    for q in range(1, each):
        own = jnp.where(me % each == q, pltpu.roll(total, 128 - q * lanes, 1), own)
    gain_out[...] = own[:, :lanes]

    def finish_last(k, carry):
        out[:, cols(k)] = give(1, k).astype(BF16)
        return carry

    lax.fori_loop(0, CHUNKS, finish_last, 0)

    for k in range(CHUNKS):
        for g in range(2):
            wait_send(2, g, k, send_src)
            wait_send(3, g, k, send_exp)


def shards(tokens, cotangent, routes, route_gates, norm_gain, gate_matrix, up_matrix, down_matrix):
    experts, dps = lax.axis_size("expert"), lax.axis_size("dp")
    rows, features = tokens.shape
    inner = gate_matrix.shape[2]
    cap = 2 * rows * routes.shape[1] // experts
    width = features // CHUNKS
    dims = (rows, features, inner, experts, cap, dps)
    hbm = pl.BlockSpec(memory_space=pltpu.HBM)
    vmem = pl.BlockSpec(memory_space=pltpu.VMEM)
    dma = pltpu.SemaphoreType.DMA
    half = experts * cap // 2
    slab = lambda: pltpu.VMEM((2, CHUNKS, half, width), BF16)
    weight = lambda: pltpu.VMEM((CHUNKS, width, inner), BF16)
    grads, gain_part = pl.pallas_call(
        functools.partial(kernel, dims),
        out_shape=(
            jax.ShapeDtypeStruct((rows, features), BF16),
            jax.ShapeDtypeStruct((1, features // (experts * dps)), F32),
        ),
        in_specs=[hbm] * 8,
        out_specs=(vmem, vmem),
        scratch_shapes=[
            slab(), slab(), slab(), slab(),
            pltpu.VMEM((CHUNKS, rows, width), BF16),
            pltpu.VMEM((CHUNKS, rows, width), BF16),
            pltpu.VMEM((2, rows), jnp.int32),
            pltpu.VMEM((2, rows), F32),
            pltpu.VMEM((1, features), F32),
            weight(), weight(), weight(),
            pltpu.VMEM((CHUNKS, rows, width), F32),
            pltpu.VMEM((2, half, inner), F32),
            pltpu.VMEM((2, half, inner), F32),
            pltpu.VMEM((2, half, inner), F32),
            pltpu.VMEM((2, half, inner), BF16),
            pltpu.VMEM((2, half, inner), BF16),
            pltpu.VMEM((2, half, 2 * rows), BF16),
            pltpu.VMEM((2, 2 * rows, half), BF16),
            pltpu.VMEM((dps, 1, features // dps), F32),
            pltpu.VMEM((dps, 1, features // dps), F32),
            pltpu.VMEM((features // dps // 128, 1, 128), F32),
            pltpu.VMEM((experts, 1, 128), F32),
            dma((2, CHUNKS)),
            dma((3,)),
            dma((3, CHUNKS)),
            dma((4, 2, CHUNKS)),
            dma((4, 2, CHUNKS)),
            dma((4,)),
        ],
        compiler_params=pltpu.CompilerParams(
            collective_id=0, has_side_effects=True, vmem_limit_bytes=50 * 2**20
        ),
        name="routed_experts",
    )(
        *(
            pltpu.with_memory_space_constraint(operand, pltpu.HBM)
            for operand in (
                tokens, cotangent, routes.T, route_gates.T, norm_gain.reshape(1, features),
                gate_matrix[0], up_matrix[0], down_matrix[0],
            )
        )
    )
    return grads, gain_part.reshape(-1)


def solution(mesh):
    placed = (
        P(("dp", "expert"), None),
        P(("dp", "expert"), None),
        P(("dp", "expert"), None),
        P(("dp", "expert"), None),
        P(),
        P("expert", None, None),
        P("expert", None, None),
        P("expert", None, None),
    )
    return jax.shard_map(
        shards,
        mesh=mesh,
        in_specs=placed,
        out_specs=(P(("dp", "expert"), None), P(("dp", "expert"))),
        check_vma=False,
    )
```

```python
import functools
import jax
import jax.numpy as jnp
from jax import lax
from jax.experimental import pallas as pl
from jax.experimental.pallas import tpu as pltpu
from jax.sharding import PartitionSpec as P

MESH = pl.DeviceIdType.MESH
CHUNKS = 8
F32 = jnp.float32
BF16 = jnp.bfloat16
NT = (((1,), (1,)), ((), ()))


def peer_offsets():
    offsets = [(dz, dx, dc) for dz in range(4) for dx in range(4) for dc in range(2)][1:]
    near = lambda d: min(d, 4 - d)
    return sorted(offsets, key=lambda o: -(near(o[0]) + near(o[1])))


def dot(a, b):
    return jnp.dot(a, b, preferred_element_type=F32)


def kernel(
    dims,
    tokens, cotangent, routes_in, gates_in, gain_in, gate_w, up_w, down_w,
    out, gain_out,
    send_src, recv_exp, send_exp, recv_src,
    tok, cot, routes, gates, gain, wg, wu, wd,
    residual, grads, far, far_routes, far_gates, acc_a, acc_b, acc_c, half_a, half_b,
    place, slot_gate, pick,
    gsend, grecv, gsum, gall,
    load_sem, small_sem, weight_sem, send_sem, recv_sem, line_send, line_recv, table_sem, gain_sem,
):
    rows, features, inner, experts, cap, dps = dims
    half = experts * cap // 2
    width = features // CHUNKS
    me = lax.axis_index("expert")
    dp = lax.axis_index("dp")
    z, x, c = me // 8, (me // 2) % 4, me % 2
    groups = [
        [
            ((z + dz) % 4) * 8 + ((x + dx) % 4) * 2 + (c + dc) % 2
            for dz, dx, dc in peer_offsets()
            if dc == g
        ]
        for g in range(2)
    ]
    peers = groups[0] + groups[1]

    def cols(k):
        return pl.ds(pl.multiple_of(k * width, width), width)

    def block(e):
        return pl.ds(pl.multiple_of(e // 2 * cap, cap), cap)

    def tok_copy(k):
        return pltpu.make_async_copy(tokens.at[:, cols(k)], tok.at[k], load_sem.at[0, k])

    def cot_copy(k):
        return pltpu.make_async_copy(cotangent.at[:, cols(k)], cot.at[k], load_sem.at[1, k])

    def weight_copy(which, k):
        src, dst = ((gate_w, wg), (up_w, wu), (down_w, wd))[which]
        return pltpu.make_async_copy(src.at[cols(k), :], dst.at[k], weight_sem.at[which, k])

    barrier = pltpu.get_barrier_semaphore()
    for t in peers:
        pl.semaphore_signal(barrier, inc=1, device_id=(dp, t), device_id_type=MESH)
    for s in range(1, dps):
        pl.semaphore_signal(barrier, inc=1, device_id=((dp + s) % dps, me), device_id_type=MESH)

    small = [
        pltpu.make_async_copy(src, dst, small_sem.at[i])
        for i, (src, dst) in enumerate(((routes_in, routes), (gates_in, gates), (gain_in, gain)))
    ]
    for copy in small:
        copy.start()
    for k in range(CHUNKS):
        tok_copy(k).start()

    sub = lax.broadcasted_iota(jnp.int32, (rows, rows), 0)
    lane = lax.broadcasted_iota(jnp.int32, (rows, rows), 1)
    lane_f, sub_f = lane.astype(F32), sub.astype(F32)
    later = jnp.where(sub < lane, 1.0, 0.0).astype(BF16)
    z_f, x_f, c_f = z.astype(F32), x.astype(F32), c.astype(F32)

    def column(row):
        return jnp.sum(jnp.where(sub == lane, row, 0.0), axis=1, keepdims=True)

    def rows_of(ref):
        values = ref[...].astype(F32)
        return [values[j : j + 1, :] for j in range(2)]

    def fill_place(named, scales, lines, p):
        hot = [jnp.where(row == sub_f, 1.0, 0.0) for row in named]
        before = dot((hot[0] + hot[1]).astype(BF16), later)
        hits = {line: [] for line in lines}
        for j in range(2):
            rank = jnp.sum(before * hot[j], axis=0, keepdims=True)
            chip = jnp.floor(named[j] * 0.5)
            far_core = jnp.where(named[j] - 2.0 * chip == c_f, 0.0, 64.0)
            z_e = jnp.floor(chip * 0.25)
            x_e = chip - 4.0 * z_e
            for line in lines:
                mine, place_on = ((z_e == z_f, x_e), (x_e == x_f, z_e))[line]
                slot = jnp.where(mine, far_core + place_on * cap + rank, -1.0)
                hits[line].append(jnp.where(slot == sub_f, 1.0, 0.0))
        for line in lines:
            place[line, p] = (hits[line][0] + hits[line][1]).astype(BF16)
            weight = jnp.sum(
                hits[line][0] * scales[0] + hits[line][1] * scales[1], axis=1, keepdims=True
            )
            slot_gate[line, p] = jnp.broadcast_to(weight, (rows, rows))

    for copy in small:
        copy.wait()

    pl.semaphore_wait(barrier, experts - 1 + dps - 1)

    def send(phase, g, k, src, dst):
        if g == 0:
            pltpu.make_async_copy(
                src.at[g, k, block(me)], dst.at[g, k, block(me)], recv_sem.at[phase, g, k]
            ).start()
        for t in groups[g]:
            pltpu.make_async_remote_copy(
                src_ref=src.at[g, k, block(t)],
                dst_ref=dst.at[g, k, block(me)],
                send_sem=send_sem.at[phase, g, k],
                recv_sem=recv_sem.at[phase, g, k],
                device_id=(dp, t),
                device_id_type=MESH,
            ).start()

    def wait_recv(phase, g, k, dst):
        pltpu.make_async_copy(dst.at[g, k], dst.at[g, k], recv_sem.at[phase, g, k]).wait()

    def wait_send(phase, g, k, src):
        part = src.at[g, k, pl.ds(0, cap * len(groups[g]))]
        pltpu.make_async_copy(part, part, send_sem.at[phase, g, k]).wait()

    def stream(phase, g, make, src, dst):
        make(0)

        def step(k, carry):
            make(k)
            send(phase, g, k - 1, src, dst)
            return carry

        lax.fori_loop(1, CHUNKS, step, 0)
        send(phase, g, CHUNKS - 1, src, dst)

    def device(zz, xx, cc):
        return zz % 4 * 8 + xx % 4 * 2 + cc

    def on_line(line, p):
        return device(z + p, x, c) if line == 0 else device(z, x + p, c)

    def across(line, q, g):
        cc = (c + g) % 2
        return device(z, x + q, cc) if line == 0 else device(z + q, x, cc)

    def line_copy(step, k, line, d, src, dst, send, recv):
        return pltpu.make_async_remote_copy(
            src_ref=src,
            dst_ref=dst,
            send_sem=line_send.at[step, send],
            recv_sem=line_recv.at[step, k, recv],
            device_id=(dp, on_line(line, d)),
            device_id_type=MESH,
        )

    def start_line(step, k, line, held):
        for d in (1, 3):
            line_copy(step, k, line, d, held.at[k], far.at[k, 3 - d], 0, 3 - d).start()

    def wait_line(step, k, p):
        part = far.at[k, p - 1]
        pltpu.make_async_copy(part, part, line_recv.at[step, k, p - 1]).wait()

    def relay(step, k, line):
        for p, at in ((3, 0), (1, rows // 2)):
            wait_line(step, k, p)
            part = pl.ds(at, rows // 2)
            line_copy(
                step, k, line, 4 - p, far.at[k, p - 1, part], far.at[k, 1, part], 1, 1
            ).start()

    def wait_line_sends(step):
        for end in range(2):
            part = far.at[:, pl.ds(0, 2 - end)]
            pltpu.make_async_copy(part, part, line_send.at[step, end]).wait()

    def send_named(phase, g, k, line):
        for p in (0, 3, 1, 2):
            source = block(on_line(line, p))
            for q in range(4):
                axis = (x, z)[line]
                start = p * 4 * cap + (axis + q) % 4 * cap
                part = send_src.at[g, k, pl.ds(pl.multiple_of(start, cap), cap)]
                arrive = recv_exp.at[g, k, source]
                if g == 0 and q == 0:
                    pltpu.make_async_copy(part, arrive, recv_sem.at[phase, g, k]).start()
                else:
                    pltpu.make_async_remote_copy(
                        src_ref=part,
                        dst_ref=arrive,
                        send_sem=send_sem.at[phase, g, k],
                        recv_sem=recv_sem.at[phase, g, k],
                        device_id=(dp, across(line, q, g)),
                        device_id_type=MESH,
                    ).start()

    def wait_named(phase, g, k):
        part = send_src.at[g, k, pl.ds(0, cap * (12 + 4 * g))]
        pltpu.make_async_copy(part, part, send_sem.at[phase, g, k]).wait()

    def dispatch(phase, step, held):
        for line in range(2):
            relay(step, line, line)

        def choose(pair, carry):
            @pl.when(pair + 1 < CHUNKS // 2)
            def _():
                for line in range(2):
                    relay(step, 2 * pair + 2 + line, line)

            for line in range(2):
                k = 2 * pair + line
                if step == 1:
                    for g in range(2):
                        wait_named(0, g, k)
                for p in (0, 3, 1, 2):
                    if p == 2:
                        wait_line(step, k, 2)
                    source = held[k] if p == 0 else far[k, p - 1]
                    chosen = dot(place[line, p], source)
                    if step == 1:
                        chosen = chosen * slot_gate[line, p][:, :1]
                    chosen = chosen.astype(BF16)
                    for g in range(2):
                        send_src[g, k, pl.ds(p * 4 * cap, 4 * cap), :] = chosen[
                            g * 4 * cap : (g + 1) * 4 * cap
                        ]
                send_named(phase, 0, k, line)
            return carry

        lax.fori_loop(0, CHUNKS // 2, choose, 0)

        def send_rest(pair, carry):
            for line in range(2):
                send_named(phase, 1, 2 * pair + line, line)
            return carry

        lax.fori_loop(0, CHUNKS // 2, send_rest, 0)

    def table_copies(line, p):
        return [
            pltpu.make_async_remote_copy(
                src_ref=src,
                dst_ref=dst.at[line, 3 - p],
                send_sem=table_sem.at[i, 0],
                recv_sem=table_sem.at[i, 1],
                device_id=(dp, on_line(line, p)),
                device_id_type=MESH,
            )
            for i, (src, dst) in enumerate(((routes, far_routes), (gates, far_gates)))
        ]

    for line in range(2):
        for p in range(1, 4):
            for copy in table_copies(line, p):
                copy.start()

    def start_tokens(pair, carry):
        for line in range(2):
            k = 2 * pair + line
            tok_copy(k).wait()
            start_line(0, k, line, tok)
        return carry

    lax.fori_loop(0, CHUNKS // 2, start_tokens, 0)
    for k in range(CHUNKS):
        weight_copy(0, k).start()
        weight_copy(1, k).start()
    for k in range(CHUNKS):
        weight_copy(2, k).start()
        cot_copy(k).start()

    named_row = rows_of(routes)
    fill_place(named_row, rows_of(gates), (0, 1), 0)
    for i, table in enumerate((far_routes, far_gates)):
        for end in range(2):
            pltpu.make_async_copy(table, table, table_sem.at[i, end]).wait()
    for line in range(2):
        for p in range(1, 4):
            fill_place(
                rows_of(far_routes.at[line, p - 1]), rows_of(far_gates.at[line, p - 1]), (line,), p
            )
    dispatch(0, 0, tok)
    wait_line_sends(0)

    core = c.astype(F32)

    def base(expert):
        chip = jnp.floor(expert * 0.5)
        return chip * cap + jnp.where(expert - 2.0 * chip == core, 0.0, float(half))

    named_col = [column(row) for row in named_row]
    hot_col = [jnp.where(named_col[j] == lane_f, 1.0, 0.0) for j in range(2)]
    earlier = jnp.where(lane < sub, 1.0, 0.0).astype(BF16)
    before_col = dot(earlier, (hot_col[0] + hot_col[1]).astype(BF16))
    slot_lane = lax.broadcasted_iota(jnp.int32, (rows, half), 1).astype(F32)
    for j in range(2):
        slot_col = base(named_col[j]) + jnp.sum(before_col * hot_col[j], axis=1, keepdims=True)
        for g in range(2):
            hit = slot_col - g * half == slot_lane
            pick[g, pl.ds(j * rows, rows), :] = jnp.where(hit, 1.0, 0.0).astype(BF16)

    acc_a[...] = jnp.zeros_like(acc_a)
    acc_b[...] = jnp.zeros_like(acc_b)
    acc_c[...] = jnp.zeros_like(acc_c)

    for g in range(2):

        def project(k, carry):
            if g == 0:
                weight_copy(0, k).wait()
                weight_copy(1, k).wait()
            wait_recv(0, g, k, recv_exp)
            acc_a[g] += dot(recv_exp[g, k], wg[k])
            acc_b[g] += dot(recv_exp[g, k], wu[k])
            return carry

        lax.fori_loop(0, CHUNKS, project, 0)
        pre_gate = acc_a[g]
        half_a[g] = (pre_gate * jax.nn.sigmoid(pre_gate) * acc_b[g]).astype(BF16)

        def make_out(k):
            if g == 0:
                weight_copy(2, k).wait()
            send_exp[g, k] = lax.dot_general(
                half_a[g], wd[k], NT, preferred_element_type=F32
            ).astype(BF16)

        stream(1, g, make_out, send_exp, recv_src)

    scale = [column(gates[pl.ds(j, 1), :]) for j in range(2)]

    def take(g, k):
        taken = dot(pick[g], recv_src[g, k])
        return scale[0] * taken[:rows] + scale[1] * taken[rows:]

    def combine_first(k, carry):
        wait_recv(1, 0, k, recv_src)
        residual[k] = tok[k].astype(F32) + take(0, k)
        return carry

    lax.fori_loop(0, CHUNKS, combine_first, 0)

    def combine_last(k, carry):
        squares, products = carry
        cot_copy(k).wait()
        wait_recv(1, 1, k, recv_src)
        row = residual[k] + take(1, k)
        residual[k] = row
        scaled = cot[k].astype(F32) * gain[:, cols(k)]
        squares = squares + jnp.sum(row * row, axis=1, keepdims=True)
        products = products + jnp.sum(scaled * row, axis=1, keepdims=True)
        return squares, products

    zero = jnp.zeros((rows, 1), F32)
    squares, products = lax.fori_loop(0, CHUNKS, combine_last, (zero, zero))
    inverse = lax.rsqrt(squares * (1.0 / features) + 1e-06)
    mean = products * inverse * (1.0 / features)

    per_dp = features // dps

    def make_grad(pair, carry):
        for line in range(2):
            k = 2 * pair + line
            normed = residual[k] * inverse
            grad = inverse * (cot[k].astype(F32) * gain[:, cols(k)] - normed * mean)
            grads[k] = grad.astype(BF16)
            at = k * width
            gsend[at // per_dp, :, pl.ds(pl.multiple_of(at % per_dp, width), width)] = jnp.sum(
                cot[k].astype(F32) * normed, axis=0, keepdims=True
            )
            residual[k] = grad
            if line == 1:
                start_line(1, k - 1, 0, grads)
        start_line(1, 2 * pair + 1, 1, grads)
        return carry

    lax.fori_loop(0, CHUNKS // 2, make_grad, 0)
    dispatch(2, 1, grads)

    def gain_copy(s):
        other = (dp + s) % dps
        return pltpu.make_async_remote_copy(
            src_ref=gsend.at[other],
            dst_ref=grecv.at[dp],
            send_sem=gain_sem.at[0],
            recv_sem=gain_sem.at[1],
            device_id=(other, me),
            device_id_type=MESH,
        )

    for s in range(1, dps):
        gain_copy(s).start()
    grecv[dp] = gsend[dp]

    for g in range(2):

        def take_grad(k, carry):
            wait_recv(2, g, k, recv_exp)
            acc_c[g] += dot(recv_exp[g, k], wd[k])
            return carry

        lax.fori_loop(0, CHUNKS, take_grad, 0)
        pre_gate = acc_a[g]
        sigmoid_gate = jax.nn.sigmoid(pre_gate)
        hidden_grad = acc_c[g]
        half_a[g] = (
            hidden_grad * acc_b[g] * sigmoid_gate * (1.0 + pre_gate * (1.0 - sigmoid_gate))
        ).astype(BF16)
        half_b[g] = (hidden_grad * pre_gate * sigmoid_gate).astype(BF16)

        def make_back(k):
            wait_send(1, g, k, send_exp)
            back = lax.dot_general(half_a[g], wg[k], NT, preferred_element_type=F32)
            back = back + lax.dot_general(half_b[g], wu[k], NT, preferred_element_type=F32)
            send_exp[g, k] = back.astype(BF16)

        stream(3, g, make_back, send_exp, recv_src)

    arrived = grecv.at[pl.ds(0, dps - 1)]
    for s in range(2):
        pltpu.make_async_copy(arrived, arrived, gain_sem.at[s]).wait()
    part = grecv[0]
    for s in range(1, dps):
        part = part + grecv[s]
    tiles = per_dp // 128
    each = experts // tiles
    for b in range(tiles):
        gsum[b] = part[:, b * 128 : (b + 1) * 128]

    for t in peers:
        pltpu.make_async_remote_copy(
            src_ref=gsum.at[t // each],
            dst_ref=gall.at[me],
            send_sem=gain_sem.at[2],
            recv_sem=gain_sem.at[3],
            device_id=(dp, t),
            device_id_type=MESH,
        ).start()
    gall[me] = gsum[me // each]

    def give(g, k):
        pair = pick[g, pl.ds(0, rows), :] + pick[g, pl.ds(rows, rows), :]
        wait_recv(3, g, k, recv_src)
        return residual[k] + dot(pair, recv_src[g, k])

    def finish_first(k, carry):
        residual[k] = give(0, k)
        return carry

    lax.fori_loop(0, CHUNKS, finish_first, 0)

    arrived = gall.at[pl.ds(0, experts - 1)]
    for s in range(2, 4):
        pltpu.make_async_copy(arrived, arrived, gain_sem.at[s]).wait()
    total = jnp.sum(gall[...], axis=0)
    lanes = 128 // each
    own = total
    for q in range(1, each):
        own = jnp.where(me % each == q, pltpu.roll(total, 128 - q * lanes, 1), own)
    gain_out[...] = own[:, :lanes]

    def finish_last(k, carry):
        out[:, cols(k)] = give(1, k).astype(BF16)
        return carry

    lax.fori_loop(0, CHUNKS, finish_last, 0)

    for k in range(CHUNKS):
        for g in range(2):
            wait_named(2, g, k)
            wait_send(3, g, k, send_exp)
    wait_line_sends(1)


def shards(tokens, cotangent, routes, route_gates, norm_gain, gate_matrix, up_matrix, down_matrix):
    experts, dps = lax.axis_size("expert"), lax.axis_size("dp")
    rows, features = tokens.shape
    inner = gate_matrix.shape[2]
    cap = 2 * rows * routes.shape[1] // experts
    width = features // CHUNKS
    dims = (rows, features, inner, experts, cap, dps)
    hbm = pl.BlockSpec(memory_space=pltpu.HBM)
    vmem = pl.BlockSpec(memory_space=pltpu.VMEM)
    dma = pltpu.SemaphoreType.DMA
    half = experts * cap // 2
    slab = lambda: pltpu.VMEM((2, CHUNKS, half, width), BF16)
    weight = lambda: pltpu.VMEM((CHUNKS, width, inner), BF16)
    grads, gain_part = pl.pallas_call(
        functools.partial(kernel, dims),
        out_shape=(
            jax.ShapeDtypeStruct((rows, features), BF16),
            jax.ShapeDtypeStruct((1, features // (experts * dps)), F32),
        ),
        in_specs=[hbm] * 8,
        out_specs=(vmem, vmem),
        scratch_shapes=[
            slab(), slab(), slab(), slab(),
            pltpu.VMEM((CHUNKS, rows, width), BF16),
            pltpu.VMEM((CHUNKS, rows, width), BF16),
            pltpu.VMEM((2, rows), jnp.int32),
            pltpu.VMEM((2, rows), F32),
            pltpu.VMEM((1, features), F32),
            weight(), weight(), weight(),
            pltpu.VMEM((CHUNKS, rows, width), F32),
            pltpu.VMEM((CHUNKS, rows, width), BF16),
            pltpu.VMEM((CHUNKS, 3, rows, width), BF16),
            pltpu.VMEM((2, 3, 2, rows), jnp.int32),
            pltpu.VMEM((2, 3, 2, rows), F32),
            pltpu.VMEM((2, half, inner), F32),
            pltpu.VMEM((2, half, inner), F32),
            pltpu.VMEM((2, half, inner), F32),
            pltpu.VMEM((2, half, inner), BF16),
            pltpu.VMEM((2, half, inner), BF16),
            pltpu.VMEM((2, 4, rows, rows), BF16),
            pltpu.VMEM((2, 4, rows, rows), F32),
            pltpu.VMEM((2, 2 * rows, half), BF16),
            pltpu.VMEM((dps, 1, features // dps), F32),
            pltpu.VMEM((dps, 1, features // dps), F32),
            pltpu.VMEM((features // dps // 128, 1, 128), F32),
            pltpu.VMEM((experts, 1, 128), F32),
            dma((2, CHUNKS)),
            dma((3,)),
            dma((3, CHUNKS)),
            dma((4, 2, CHUNKS)),
            dma((4, 2, CHUNKS)),
            dma((2, 2)),
            dma((2, CHUNKS, 3)),
            dma((2, 2)),
            dma((4,)),
        ],
        compiler_params=pltpu.CompilerParams(
            collective_id=0, has_side_effects=True, vmem_limit_bytes=52 * 2**20
        ),
        name="routed_experts",
    )(
        *(
            pltpu.with_memory_space_constraint(operand, pltpu.HBM)
            for operand in (
                tokens, cotangent, routes.T, route_gates.T, norm_gain.reshape(1, features),
                gate_matrix[0], up_matrix[0], down_matrix[0],
            )
        )
    )
    return grads, gain_part.reshape(-1)


def solution(mesh):
    placed = (
        P(("dp", "expert"), None),
        P(("dp", "expert"), None),
        P(("dp", "expert"), None),
        P(("dp", "expert"), None),
        P(),
        P("expert", None, None),
        P("expert", None, None),
        P("expert", None, None),
    )
    return jax.shard_map(
        shards,
        mesh=mesh,
        in_specs=placed,
        out_specs=(P(("dp", "expert"), None), P(("dp", "expert"))),
        check_vma=False,
    )
```

```python
import functools
import jax
import jax.numpy as jnp
from jax import lax
from jax.experimental import pallas as pl
from jax.experimental.pallas import tpu as pltpu
from jax.sharding import PartitionSpec as P

MESH = pl.DeviceIdType.MESH
CHUNKS = 8
F32 = jnp.float32
BF16 = jnp.bfloat16
NT = (((1,), (1,)), ((), ()))


def peer_offsets():
    offsets = [(dz, dx, dc) for dz in range(4) for dx in range(4) for dc in range(2)][1:]
    near = lambda d: min(d, 4 - d)
    return sorted(offsets, key=lambda o: -(near(o[0]) + near(o[1])))


def dot(a, b):
    return jnp.dot(a, b, preferred_element_type=F32)


def kernel(
    dims,
    tokens, cotangent, routes_in, gates_in, gain_in, gate_w, up_w, down_w,
    out, gain_out,
    send_src, recv_exp, send_exp, recv_src,
    tok, cot, routes, gates, gain, wg, wu, wd,
    residual, grads, far, far_routes, far_gates, acc_a, acc_b, acc_c, half_a, half_b,
    place, slot_gate, pick,
    gsend, grecv, gsum, gall,
    load_sem, small_sem, weight_sem, send_sem, recv_sem, line_send, line_recv, table_sem, gain_sem,
):
    rows, features, inner, experts, cap, dps = dims
    half = experts * cap // 2
    width = features // CHUNKS
    me = lax.axis_index("expert")
    dp = lax.axis_index("dp")
    z, x, c = me // 8, (me // 2) % 4, me % 2
    groups = [
        [
            ((z + dz) % 4) * 8 + ((x + dx) % 4) * 2 + (c + dc) % 2
            for dz, dx, dc in peer_offsets()
            if dc == g
        ]
        for g in range(2)
    ]
    peers = groups[0] + groups[1]

    def cols(k):
        return pl.ds(pl.multiple_of(k * width, width), width)

    def block(e):
        return pl.ds(pl.multiple_of(e // 2 * cap, cap), cap)

    def tok_copy(k):
        return pltpu.make_async_copy(tokens.at[:, cols(k)], tok.at[k], load_sem.at[0, k])

    def cot_copy(k):
        return pltpu.make_async_copy(cotangent.at[:, cols(k)], cot.at[k], load_sem.at[1, k])

    def weight_copy(which, k):
        src, dst = ((gate_w, wg), (up_w, wu), (down_w, wd))[which]
        return pltpu.make_async_copy(src.at[cols(k), :], dst.at[k], weight_sem.at[which, k])

    barrier = pltpu.get_barrier_semaphore()
    for t in peers:
        pl.semaphore_signal(barrier, inc=1, device_id=(dp, t), device_id_type=MESH)
    for s in range(1, dps):
        pl.semaphore_signal(barrier, inc=1, device_id=((dp + s) % dps, me), device_id_type=MESH)

    small = [
        pltpu.make_async_copy(src, dst, small_sem.at[i])
        for i, (src, dst) in enumerate(((routes_in, routes), (gates_in, gates), (gain_in, gain)))
    ]
    for copy in small:
        copy.start()
    for k in range(CHUNKS):
        tok_copy(k).start()

    sub = lax.broadcasted_iota(jnp.int32, (rows, rows), 0)
    lane = lax.broadcasted_iota(jnp.int32, (rows, rows), 1)
    lane_f, sub_f = lane.astype(F32), sub.astype(F32)
    later = jnp.where(sub < lane, 1.0, 0.0).astype(BF16)
    z_f, x_f, c_f = z.astype(F32), x.astype(F32), c.astype(F32)

    def column(row):
        return jnp.sum(jnp.where(sub == lane, row, 0.0), axis=1, keepdims=True)

    def rows_of(ref):
        values = ref[...].astype(F32)
        return [values[j : j + 1, :] for j in range(2)]

    def fill_place(named, scales, lines, p):
        hot = [jnp.where(row == sub_f, 1.0, 0.0) for row in named]
        before = dot((hot[0] + hot[1]).astype(BF16), later)
        hits = {line: [] for line in lines}
        for j in range(2):
            rank = jnp.sum(before * hot[j], axis=0, keepdims=True)
            chip = jnp.floor(named[j] * 0.5)
            far_core = jnp.where(named[j] - 2.0 * chip == c_f, 0.0, 64.0)
            z_e = jnp.floor(chip * 0.25)
            x_e = chip - 4.0 * z_e
            for line in lines:
                mine, place_on = ((z_e == z_f, x_e), (x_e == x_f, z_e))[line]
                slot = jnp.where(mine, far_core + place_on * cap + rank, -1.0)
                hits[line].append(jnp.where(slot == sub_f, 1.0, 0.0))
        for line in lines:
            place[line, p] = (hits[line][0] + hits[line][1]).astype(BF16)
            weight = jnp.sum(
                hits[line][0] * scales[0] + hits[line][1] * scales[1], axis=1, keepdims=True
            )
            slot_gate[line, p] = jnp.broadcast_to(weight, (rows, rows))

    for copy in small:
        copy.wait()

    pl.semaphore_wait(barrier, experts - 1 + dps - 1)

    def send(phase, g, k, src, dst):
        if g == 0:
            pltpu.make_async_copy(
                src.at[g, k, block(me)], dst.at[g, k, block(me)], recv_sem.at[phase, g, k]
            ).start()
        for t in groups[g]:
            pltpu.make_async_remote_copy(
                src_ref=src.at[g, k, block(t)],
                dst_ref=dst.at[g, k, block(me)],
                send_sem=send_sem.at[phase, g, k],
                recv_sem=recv_sem.at[phase, g, k],
                device_id=(dp, t),
                device_id_type=MESH,
            ).start()

    def wait_recv(phase, g, k, dst):
        pltpu.make_async_copy(dst.at[g, k], dst.at[g, k], recv_sem.at[phase, g, k]).wait()

    def wait_send(phase, g, k, src):
        part = src.at[g, k, pl.ds(0, cap * len(groups[g]))]
        pltpu.make_async_copy(part, part, send_sem.at[phase, g, k]).wait()

    def stream(phase, g, make, src, dst):
        make(0)

        def step(k, carry):
            make(k)
            send(phase, g, k - 1, src, dst)
            return carry

        lax.fori_loop(1, CHUNKS, step, 0)
        send(phase, g, CHUNKS - 1, src, dst)

    def device(zz, xx, cc):
        return zz % 4 * 8 + xx % 4 * 2 + cc

    def on_line(line, p):
        return device(z + p, x, c) if line == 0 else device(z, x + p, c)

    def across(line, q, g):
        cc = (c + g) % 2
        return device(z, x + q, cc) if line == 0 else device(z + q, x, cc)

    def line_copy(step, k, line, d, src, dst, send, recv):
        return pltpu.make_async_remote_copy(
            src_ref=src,
            dst_ref=dst,
            send_sem=line_send.at[step, send],
            recv_sem=line_recv.at[step, k, recv],
            device_id=(dp, on_line(line, d)),
            device_id_type=MESH,
        )

    def start_line(step, k, line, held):
        for d in (1, 3):
            line_copy(step, k, line, d, held.at[k], far.at[k, 3 - d], 0, 3 - d).start()

    def wait_line(step, k, p):
        part = far.at[k, p - 1]
        pltpu.make_async_copy(part, part, line_recv.at[step, k, p - 1]).wait()

    def relay(step, k, line):
        for p, at in ((3, 0), (1, rows // 2)):
            wait_line(step, k, p)
            part = pl.ds(at, rows // 2)
            line_copy(
                step, k, line, 4 - p, far.at[k, p - 1, part], far.at[k, 1, part], 1, 1
            ).start()

    def wait_line_sends(step):
        for end in range(2):
            part = far.at[:, pl.ds(0, 2 - end)]
            pltpu.make_async_copy(part, part, line_send.at[step, end]).wait()

    def send_named(phase, g, k, line):
        for p in (0, 3, 1, 2):
            source = block(on_line(line, p))
            for q in range(4):
                axis = (x, z)[line]
                start = p * 4 * cap + (axis + q) % 4 * cap
                part = send_src.at[g, k, pl.ds(pl.multiple_of(start, cap), cap)]
                arrive = recv_exp.at[g, k, source]
                if g == 0 and q == 0:
                    pltpu.make_async_copy(part, arrive, recv_sem.at[phase, g, k]).start()
                else:
                    pltpu.make_async_remote_copy(
                        src_ref=part,
                        dst_ref=arrive,
                        send_sem=send_sem.at[phase, g, k],
                        recv_sem=recv_sem.at[phase, g, k],
                        device_id=(dp, across(line, q, g)),
                        device_id_type=MESH,
                    ).start()

    def wait_named(phase, g, k):
        part = send_src.at[g, k, pl.ds(0, cap * (12 + 4 * g))]
        pltpu.make_async_copy(part, part, send_sem.at[phase, g, k]).wait()

    def dispatch(phase, step, held):
        for k in range(4):
            relay(step, k, k % 2)

        def choose(pair, carry):
            @pl.when(pair + 2 < CHUNKS // 2)
            def _():
                for line in range(2):
                    relay(step, 2 * pair + 4 + line, line)

            for line in range(2):
                k = 2 * pair + line
                if step == 1:
                    for g in range(2):
                        wait_named(0, g, k)
                for p in (0, 3, 1, 2):
                    if p == 2:
                        wait_line(step, k, 2)
                    source = held[k] if p == 0 else far[k, p - 1]
                    chosen = dot(place[line, p], source)
                    if step == 1:
                        chosen = chosen * slot_gate[line, p][:, :1]
                    chosen = chosen.astype(BF16)
                    for g in range(2):
                        send_src[g, k, pl.ds(p * 4 * cap, 4 * cap), :] = chosen[
                            g * 4 * cap : (g + 1) * 4 * cap
                        ]
                send_named(phase, 0, k, line)
            return carry

        lax.fori_loop(0, CHUNKS // 2, choose, 0)

        def send_rest(pair, carry):
            for line in range(2):
                send_named(phase, 1, 2 * pair + line, line)
            return carry

        lax.fori_loop(0, CHUNKS // 2, send_rest, 0)

    def table_copies(line, p):
        return [
            pltpu.make_async_remote_copy(
                src_ref=src,
                dst_ref=dst.at[line, 3 - p],
                send_sem=table_sem.at[i, 0],
                recv_sem=table_sem.at[i, 1],
                device_id=(dp, on_line(line, p)),
                device_id_type=MESH,
            )
            for i, (src, dst) in enumerate(((routes, far_routes), (gates, far_gates)))
        ]

    for line in range(2):
        for p in range(1, 4):
            for copy in table_copies(line, p):
                copy.start()

    def start_tokens(pair, carry):
        for line in range(2):
            k = 2 * pair + line
            tok_copy(k).wait()
            start_line(0, k, line, tok)
        return carry

    lax.fori_loop(0, CHUNKS // 2, start_tokens, 0)
    for k in range(CHUNKS):
        weight_copy(0, k).start()
        weight_copy(1, k).start()
    for k in range(CHUNKS):
        weight_copy(2, k).start()
        cot_copy(k).start()

    named_row = rows_of(routes)
    fill_place(named_row, rows_of(gates), (0, 1), 0)
    for i, table in enumerate((far_routes, far_gates)):
        for end in range(2):
            pltpu.make_async_copy(table, table, table_sem.at[i, end]).wait()
    for line in range(2):
        for p in range(1, 4):
            fill_place(
                rows_of(far_routes.at[line, p - 1]), rows_of(far_gates.at[line, p - 1]), (line,), p
            )
    dispatch(0, 0, tok)
    wait_line_sends(0)

    core = c.astype(F32)

    def base(expert):
        chip = jnp.floor(expert * 0.5)
        return chip * cap + jnp.where(expert - 2.0 * chip == core, 0.0, float(half))

    named_col = [column(row) for row in named_row]
    hot_col = [jnp.where(named_col[j] == lane_f, 1.0, 0.0) for j in range(2)]
    earlier = jnp.where(lane < sub, 1.0, 0.0).astype(BF16)
    before_col = dot(earlier, (hot_col[0] + hot_col[1]).astype(BF16))
    slot_lane = lax.broadcasted_iota(jnp.int32, (rows, half), 1).astype(F32)
    for j in range(2):
        slot_col = base(named_col[j]) + jnp.sum(before_col * hot_col[j], axis=1, keepdims=True)
        for g in range(2):
            hit = slot_col - g * half == slot_lane
            pick[g, pl.ds(j * rows, rows), :] = jnp.where(hit, 1.0, 0.0).astype(BF16)

    acc_a[...] = jnp.zeros_like(acc_a)
    acc_b[...] = jnp.zeros_like(acc_b)
    acc_c[...] = jnp.zeros_like(acc_c)

    for g in range(2):

        def project(k, carry):
            if g == 0:
                weight_copy(0, k).wait()
                weight_copy(1, k).wait()
            wait_recv(0, g, k, recv_exp)
            acc_a[g] += dot(recv_exp[g, k], wg[k])
            acc_b[g] += dot(recv_exp[g, k], wu[k])
            return carry

        lax.fori_loop(0, CHUNKS, project, 0)
        pre_gate = acc_a[g]
        half_a[g] = (pre_gate * jax.nn.sigmoid(pre_gate) * acc_b[g]).astype(BF16)

        def make_out(k):
            if g == 0:
                weight_copy(2, k).wait()
            send_exp[g, k] = lax.dot_general(
                half_a[g], wd[k], NT, preferred_element_type=F32
            ).astype(BF16)

        stream(1, g, make_out, send_exp, recv_src)

    scale = [column(gates[pl.ds(j, 1), :]) for j in range(2)]

    def take(g, k):
        taken = dot(pick[g], recv_src[g, k])
        return scale[0] * taken[:rows] + scale[1] * taken[rows:]

    def combine_first(k, carry):
        wait_recv(1, 0, k, recv_src)
        residual[k] = tok[k].astype(F32) + take(0, k)
        return carry

    lax.fori_loop(0, CHUNKS, combine_first, 0)

    def combine_last(k, carry):
        squares, products = carry
        cot_copy(k).wait()
        wait_recv(1, 1, k, recv_src)
        row = residual[k] + take(1, k)
        residual[k] = row
        scaled = cot[k].astype(F32) * gain[:, cols(k)]
        squares = squares + jnp.sum(row * row, axis=1, keepdims=True)
        products = products + jnp.sum(scaled * row, axis=1, keepdims=True)
        return squares, products

    zero = jnp.zeros((rows, 1), F32)
    squares, products = lax.fori_loop(0, CHUNKS, combine_last, (zero, zero))
    inverse = lax.rsqrt(squares * (1.0 / features) + 1e-06)
    mean = products * inverse * (1.0 / features)

    per_dp = features // dps

    def make_grad(pair, carry):
        for line in range(2):
            k = 2 * pair + line
            normed = residual[k] * inverse
            grad = inverse * (cot[k].astype(F32) * gain[:, cols(k)] - normed * mean)
            grads[k] = grad.astype(BF16)
            at = k * width
            gsend[at // per_dp, :, pl.ds(pl.multiple_of(at % per_dp, width), width)] = jnp.sum(
                cot[k].astype(F32) * normed, axis=0, keepdims=True
            )
            residual[k] = grad
            if line == 1:
                start_line(1, k - 1, 0, grads)
        start_line(1, 2 * pair + 1, 1, grads)
        return carry

    lax.fori_loop(0, CHUNKS // 2, make_grad, 0)
    dispatch(2, 1, grads)

    def gain_copy(s):
        other = (dp + s) % dps
        return pltpu.make_async_remote_copy(
            src_ref=gsend.at[other],
            dst_ref=grecv.at[dp],
            send_sem=gain_sem.at[0],
            recv_sem=gain_sem.at[1],
            device_id=(other, me),
            device_id_type=MESH,
        )

    for s in range(1, dps):
        gain_copy(s).start()
    grecv[dp] = gsend[dp]

    for g in range(2):

        def take_grad(k, carry):
            wait_recv(2, g, k, recv_exp)
            acc_c[g] += dot(recv_exp[g, k], wd[k])
            return carry

        lax.fori_loop(0, CHUNKS, take_grad, 0)
        pre_gate = acc_a[g]
        sigmoid_gate = jax.nn.sigmoid(pre_gate)
        hidden_grad = acc_c[g]
        half_a[g] = (
            hidden_grad * acc_b[g] * sigmoid_gate * (1.0 + pre_gate * (1.0 - sigmoid_gate))
        ).astype(BF16)
        half_b[g] = (hidden_grad * pre_gate * sigmoid_gate).astype(BF16)

        def make_back(k):
            wait_send(1, g, k, send_exp)
            back = lax.dot_general(half_a[g], wg[k], NT, preferred_element_type=F32)
            back = back + lax.dot_general(half_b[g], wu[k], NT, preferred_element_type=F32)
            send_exp[g, k] = back.astype(BF16)

        stream(3, g, make_back, send_exp, recv_src)

    arrived = grecv.at[pl.ds(0, dps - 1)]
    for s in range(2):
        pltpu.make_async_copy(arrived, arrived, gain_sem.at[s]).wait()
    part = grecv[0]
    for s in range(1, dps):
        part = part + grecv[s]
    tiles = per_dp // 128
    each = experts // tiles
    for b in range(tiles):
        gsum[b] = part[:, b * 128 : (b + 1) * 128]

    for t in peers:
        pltpu.make_async_remote_copy(
            src_ref=gsum.at[t // each],
            dst_ref=gall.at[me],
            send_sem=gain_sem.at[2],
            recv_sem=gain_sem.at[3],
            device_id=(dp, t),
            device_id_type=MESH,
        ).start()
    gall[me] = gsum[me // each]

    def give(g, k):
        pair = pick[g, pl.ds(0, rows), :] + pick[g, pl.ds(rows, rows), :]
        wait_recv(3, g, k, recv_src)
        return residual[k] + dot(pair, recv_src[g, k])

    def finish_first(k, carry):
        residual[k] = give(0, k)
        return carry

    lax.fori_loop(0, CHUNKS, finish_first, 0)

    arrived = gall.at[pl.ds(0, experts - 1)]
    for s in range(2, 4):
        pltpu.make_async_copy(arrived, arrived, gain_sem.at[s]).wait()
    total = jnp.sum(gall[...], axis=0)
    lanes = 128 // each
    own = total
    for q in range(1, each):
        own = jnp.where(me % each == q, pltpu.roll(total, 128 - q * lanes, 1), own)
    gain_out[...] = own[:, :lanes]

    def finish_last(k, carry):
        out[:, cols(k)] = give(1, k).astype(BF16)
        return carry

    lax.fori_loop(0, CHUNKS, finish_last, 0)

    for k in range(CHUNKS):
        for g in range(2):
            wait_named(2, g, k)
            wait_send(3, g, k, send_exp)
    wait_line_sends(1)


def shards(tokens, cotangent, routes, route_gates, norm_gain, gate_matrix, up_matrix, down_matrix):
    experts, dps = lax.axis_size("expert"), lax.axis_size("dp")
    rows, features = tokens.shape
    inner = gate_matrix.shape[2]
    cap = 2 * rows * routes.shape[1] // experts
    width = features // CHUNKS
    dims = (rows, features, inner, experts, cap, dps)
    hbm = pl.BlockSpec(memory_space=pltpu.HBM)
    vmem = pl.BlockSpec(memory_space=pltpu.VMEM)
    dma = pltpu.SemaphoreType.DMA
    half = experts * cap // 2
    slab = lambda: pltpu.VMEM((2, CHUNKS, half, width), BF16)
    weight = lambda: pltpu.VMEM((CHUNKS, width, inner), BF16)
    grads, gain_part = pl.pallas_call(
        functools.partial(kernel, dims),
        out_shape=(
            jax.ShapeDtypeStruct((rows, features), BF16),
            jax.ShapeDtypeStruct((1, features // (experts * dps)), F32),
        ),
        in_specs=[hbm] * 8,
        out_specs=(vmem, vmem),
        scratch_shapes=[
            slab(), slab(), slab(), slab(),
            pltpu.VMEM((CHUNKS, rows, width), BF16),
            pltpu.VMEM((CHUNKS, rows, width), BF16),
            pltpu.VMEM((2, rows), jnp.int32),
            pltpu.VMEM((2, rows), F32),
            pltpu.VMEM((1, features), F32),
            weight(), weight(), weight(),
            pltpu.VMEM((CHUNKS, rows, width), F32),
            pltpu.VMEM((CHUNKS, rows, width), BF16),
            pltpu.VMEM((CHUNKS, 3, rows, width), BF16),
            pltpu.VMEM((2, 3, 2, rows), jnp.int32),
            pltpu.VMEM((2, 3, 2, rows), F32),
            pltpu.VMEM((2, half, inner), F32),
            pltpu.VMEM((2, half, inner), F32),
            pltpu.VMEM((2, half, inner), F32),
            pltpu.VMEM((2, half, inner), BF16),
            pltpu.VMEM((2, half, inner), BF16),
            pltpu.VMEM((2, 4, rows, rows), BF16),
            pltpu.VMEM((2, 4, rows, rows), F32),
            pltpu.VMEM((2, 2 * rows, half), BF16),
            pltpu.VMEM((dps, 1, features // dps), F32),
            pltpu.VMEM((dps, 1, features // dps), F32),
            pltpu.VMEM((features // dps // 128, 1, 128), F32),
            pltpu.VMEM((experts, 1, 128), F32),
            dma((2, CHUNKS)),
            dma((3,)),
            dma((3, CHUNKS)),
            dma((4, 2, CHUNKS)),
            dma((4, 2, CHUNKS)),
            dma((2, 2)),
            dma((2, CHUNKS, 3)),
            dma((2, 2)),
            dma((4,)),
        ],
        compiler_params=pltpu.CompilerParams(
            collective_id=0, has_side_effects=True, vmem_limit_bytes=52 * 2**20
        ),
        name="routed_experts",
    )(
        *(
            pltpu.with_memory_space_constraint(operand, pltpu.HBM)
            for operand in (
                tokens, cotangent, routes.T, route_gates.T, norm_gain.reshape(1, features),
                gate_matrix[0], up_matrix[0], down_matrix[0],
            )
        )
    )
    return grads, gain_part.reshape(-1)


def solution(mesh):
    placed = (
        P(("dp", "expert"), None),
        P(("dp", "expert"), None),
        P(("dp", "expert"), None),
        P(("dp", "expert"), None),
        P(),
        P("expert", None, None),
        P("expert", None, None),
        P("expert", None, None),
    )
    return jax.shard_map(
        shards,
        mesh=mesh,
        in_specs=placed,
        out_specs=(P(("dp", "expert"), None), P(("dp", "expert"))),
        check_vma=False,
    )
```
